32 devices in a mesh: pln: 8 (over y, x, core), pen: 4 (over z).
Axes of the slice: x: 2, y: 2, z: 4, core: 2. Of those that a mesh axis runs over, the one named last changes fastest.
Arguments:
- block_owner: int32 [4096, 1], P(('pln', 'pen')), may hold values from 0 to 31; in each aligned block of 128 rows (0 to 127, 128 to 255, ...) at most 8 rows name the same one
- block_band: int32 [4096], P(('pln', 'pen')), may hold values from 0 to 31
- block_count: int32 [4096], P(('pln', 'pen')), may hold values from 1 to 128
- cells: int32 [4096, 128], P(('pln', 'pen')), may hold values from 0 to 8191
- offsets: float32 [4096, 2, 128], P(('pln', 'pen')), may hold values from 0 to 1
- charges: float32 [4096, 128], P(('pln', 'pen')), may hold values from -5 to 5
Outputs:
- potential: float32 [8, 1024, 1024], P('pln', 'pen')
- forces: float32 [4096, 2, 128], P(('pln', 'pen'))
The draws below stay inside these ranges and needn't reach their ends.
Inputs may be any that keep to these rules, and one draw needn't show every extreme that they name: `block_owner`: among the blocks of one device no owner is named more than 8 times, a bound that some block reaches.
All inputs are finite; a program needn't handle non-finite values.
Results may differ from the reference program's by a relative error of at most 0.0044.
Values sent between devices are 32-bit elements; how exact they have to be, the bound alone decides.
A program may use at most 64 MiB of HBM per device.

```python
import math
import jax
import jax.numpy as jnp
import numpy as np
from jax import lax

NG = 1024
BLK = 128
NB_DEV = 128
PLANES = 8
RY = 256
BANDS = 32
CAP = 8
NB_ALL = 4096
DEVICES = 32


def cell_table(key):
    return jax.random.randint(jax.random.fold_in(key, 11), (NB_ALL, BLK), 0, 8 * NG, dtype=jnp.int32)


def draw_cells(key, part):
    return cell_table(key)


def draw_charges(key, part):
    column = (cell_table(key) % NG).astype(jnp.float32)
    wave_key, angle_key, jitter_key = jax.random.split(jax.random.fold_in(key, 23), 3)
    wavenumber = jax.random.randint(wave_key, (), 9, 13, dtype=jnp.int32).astype(jnp.float32)
    start_angle = jax.random.uniform(angle_key, (), jnp.float32, -math.pi, math.pi)
    jitter = jnp.clip(jax.random.normal(jitter_key, (NB_ALL, BLK), jnp.float32), -4.0, 4.0)
    height = 0.6
    return jitter + height * jnp.cos(2.0 * math.pi * wavenumber * column / NG + start_angle)


def touch_ends(array, own_key, least, top_value):
    shape = array.shape
    place = [jax.random.randint(jax.random.fold_in(own_key, axis), (), 0, shape[axis]) for axis in range(len(shape))]
    array = array.at[tuple(place)].set(least)
    longest = shape.index(max(shape))
    place[longest] = (place[longest] + 1) % shape[longest]
    return array.at[tuple(place)].set(top_value)


def shard_levels(rng, dims, cuts, low, high):
    loudness, own = 1.0, jax.random.fold_in(rng, 6)
    for position, blocks in cuts:
        heights = jnp.exp(jax.random.uniform(jax.random.fold_in(own, position), (blocks,), jnp.float32, low / len(cuts), high / len(cuts)))
        loudness = loudness * jnp.repeat(heights, dims[position] // blocks).reshape([-1 if axis == position else 1 for axis in range(len(dims))])
    return loudness


def assign_block(rng, own, number, rows, count, top, most, lean):
    sequence = jax.random.permutation(rng, count)
    crowded, usual = shares(count, rows * top, most, lean, True), shares(count, rows * top, most, lean, False)
    places = jnp.arange(count)

    def named(sizes, rotation):
        used = int((sizes > 0).sum())
        fixed = max(1, used // 4)
        passed = fixed + (places - fixed + rotation * (used - fixed)) % max(1, count - fixed)
        return jnp.zeros((count,), jnp.int32).at[sequence[jnp.where(places < fixed, places, passed)]].set(jnp.asarray(sizes, jnp.int32))

    sizes = jnp.where(number % 4 == 0, named(crowded, number // 4), named(usual, number - number // 4 - 1))
    mixed = jax.random.permutation(jax.random.fold_in(own, 3), count)
    donor, receiver = mixed[0:count // 2 * 2:2], mixed[1:count // 2 * 2:2]
    margin = jnp.minimum(sizes[donor] - 1, most - sizes[receiver]) // 2
    margin = jnp.where((donor == sequence[0]) | (receiver == sequence[0]) | (sizes[receiver] == 0), 0, jnp.maximum(margin, 0))
    passed = jax.random.randint(jax.random.fold_in(own, 4), (count // 2,), 0, 1 << 20) % (margin + 1)
    sizes = sizes.at[donor].add(-passed).at[receiver].add(passed)
    labels = jnp.searchsorted(jnp.cumsum(sizes), jnp.arange(rows * top), side="right").astype(jnp.int32)
    table = labels.reshape(top, rows).T
    table = table[jax.random.permutation(jax.random.fold_in(own, 1), rows)]
    rotation = jax.random.randint(jax.random.fold_in(own, 2), (rows, 1), 0, top)
    return jnp.take_along_axis(table, (jnp.arange(top)[None, :] + rotation) % top, axis=1)


def shares(number_of, total, reach, lean, full):
    portions = [(1 << 20) // math.isqrt(standing ** lean) + 1 for standing in range(1, number_of + 1)]
    largest = reach if full else min(reach, max(-(-total // number_of), total * portions[0] // sum(portions)))
    least = 1 if total - largest >= number_of - 1 else 0
    given, rest = [largest] + [least] * (number_of - 1), total - largest - least * (number_of - 1)
    while rest > 0:
        free = [i for i in range(1, number_of) if given[i] < largest] or [i for i in range(1, number_of) if given[i] < reach]
        whole, budget = sum([portions[i] for i in free]), rest
        for i in free:
            extra = min(reach - given[i], max(1, budget * portions[i] // whole), rest)
            given[i] = given[i] + extra
            rest = rest - extra
    return np.array(given)


def setup_inputs(seed: int = 0) -> dict:
    keys = jax.random.split(jax.random.key(seed), 7)
    block_owner_keys = jax.random.split(jax.random.fold_in(keys[0], 1), NB_ALL // NB_DEV)
    block_owner_turns = jax.random.permutation(jax.random.fold_in(keys[0], 3), NB_ALL // NB_DEV)
    block_owner = jax.vmap(lambda own, number: assign_block(jax.random.fold_in(keys[0], 2), own, number, NB_DEV, DEVICES, 1, CAP, 2))(block_owner_keys, block_owner_turns).reshape((NB_ALL, 1))
    block_band = touch_ends(jax.random.randint(keys[1], (NB_ALL,), 0, BANDS), jax.random.fold_in(keys[1], 1), 0, BANDS - 1).astype(jnp.int32)
    block_count = touch_ends(jax.random.randint(keys[2], (NB_ALL,), 1, BLK + 1), jax.random.fold_in(keys[2], 1), 1, BLK).astype(jnp.int32)
    cells = draw_cells(jax.random.fold_in(keys[6], 71), 0)
    offsets = jnp.clip(1.0 * jax.random.uniform(keys[4], (NB_ALL, 2, BLK), jnp.float32) ** shard_levels(keys[4], (NB_ALL, 2, BLK), ((0, 32),), -0.2, 0.2), 0.0, 1.0)
    charges = draw_charges(jax.random.fold_in(keys[6], 71), 0)
    return dict(block_owner=block_owner, block_band=block_band, block_count=block_count, cells=cells, offsets=offsets, charges=charges)


screening = 2e-5


def rounded(values):
    return lax.optimization_barrier(values.astype(jnp.bfloat16)).astype(jnp.float32)


def reference(block_owner, block_band, block_count, cells, offsets, charges):
    pencils = NG // RY
    owner = block_owner[:, 0]
    slots = jnp.arange(charges.shape[1], dtype=jnp.int32)
    weight = jnp.where(slots[None, :] < block_count[:, None], charges, jnp.zeros_like(charges))
    plane = (owner // pencils)[:, None]
    row = ((owner % pencils) * RY + 8 * block_band)[:, None] + cells // NG
    column = cells % NG
    next_row = (row + 1) % NG
    next_column = (column + 1) % NG
    frac_x = offsets[:, 0]
    frac_y = offsets[:, 1]
    lower = rounded(weight * (1.0 - frac_y))
    upper = rounded(weight * frac_y)
    left = rounded(1.0 - frac_x)
    right = rounded(frac_x)

    def flat(row_idx, col_idx):
        return (plane * NG * NG + row_idx * NG + col_idx).reshape(-1)

    density = jnp.zeros((PLANES * NG * NG,), jnp.float32)
    density = density.at[flat(row, column)].add((lower * left).reshape(-1))
    density = density.at[flat(row, next_column)].add((lower * right).reshape(-1))
    density = density.at[flat(next_row, column)].add((upper * left).reshape(-1))
    density = density.at[flat(next_row, next_column)].add((upper * right).reshape(-1))
    grid = density.reshape(PLANES, NG, NG)
    freq = jnp.arange(NG).astype(jnp.float32)
    sines = jnp.sin(math.pi * freq / NG)
    green = 1.0 / (4.0 * sines[:, None] ** 2 + 4.0 * sines[None, :] ** 2 + screening)
    potential = jnp.real(jnp.fft.ifft2(jnp.fft.fft2(grid) * green)).astype(jnp.float32)

    def derivative(values, axis):
        return -(8.0 * (jnp.roll(values, -1, axis) - jnp.roll(values, 1, axis))
                 - (jnp.roll(values, -2, axis) - jnp.roll(values, 2, axis))) / 12.0

    field = jnp.stack([derivative(potential, 2), derivative(potential, 1)], axis=1)
    shape = cells.shape
    parts = []
    for comp in range(2):
        flat_field = field[:, comp].reshape(-1)
        near = left * flat_field[flat(row, column)].reshape(shape) + right * flat_field[flat(row, next_column)].reshape(shape)
        far = left * flat_field[flat(next_row, column)].reshape(shape) + right * flat_field[flat(next_row, next_column)].reshape(shape)
        parts.append(weight * ((1.0 - frac_y) * near + frac_y * far))
    forces = jnp.stack(parts, axis=1)
    return potential, forces
```

```python
import functools
import math

import jax
import jax.numpy as jnp
import numpy as np
from jax import lax
from jax.experimental import pallas as pl
from jax.experimental.pallas import tpu as pltpu
from jax.sharding import PartitionSpec as P

NG = 1024
LANES = 128
CHUNKS = NG // LANES
screening = 2e-05
VMEM_LIMIT = 48 * 1024 * 1024
UNROLL = 4


def round_up(value, step):
    return -(-value // step) * step


@functools.lru_cache(None)
def hartley_tables():
    index = np.arange(NG)
    angle = 2.0 * np.pi / NG * (index[:, None] * index[None, :] % NG)
    table = np.cos(angle) + np.sin(angle)
    high = table.astype(jnp.bfloat16)
    low = (table - high.astype(np.float64)).astype(jnp.bfloat16)
    return high, low


@functools.lru_cache(None)
def line_tables(pen_count):
    rows = NG // pen_count
    shift = 4.0 * np.sin(np.pi * np.arange(NG) / NG) ** 2 + screening
    root = 1.0 + shift / 2.0 - np.sqrt(shift + shift * shift / 4.0)
    i = np.arange(8)[:, None]

    def power(exponent):
        return root[None, :] ** (exponent + np.zeros((8, 1)))

    tiles = [
        power(7 - i),
        power(i),
        power(8),
        np.where(i >= 1, power(1), 0.0),
        np.where(i >= 2, power(2), 0.0),
        np.where(i >= 4, power(4), 0.0),
        np.where(i <= 6, power(1), 0.0),
        np.where(i <= 5, power(2), 0.0),
        np.where(i <= 3, power(4), 0.0),
        power(i + 1),
        power(8 - i),
        np.broadcast_to(1.0 / ((1.0 / root - root) * NG), (8, NG)),
        np.broadcast_to(2.0 + shift, (8, NG)),
        power(rows - 1),
    ]
    lags = np.arange(round_up(pen_count, 8))[:, None]
    tiles.append(root[None, :] ** (lags * rows) / (1.0 - root[None, :] ** NG))
    return np.concatenate(tiles, axis=0).astype(np.float32)


T_FEND, T_BEND, T_EIGHT, T_F1, T_F2, T_F4, T_B1, T_B2, T_B4, T_FC, T_BC, T_NORM, T_DIAG, T_LAST, T_LAG = range(15)


def pack_kernel(capacity, owner, band, count, cells, offsets, charges, out, target, used):
    devices = out.shape[0]
    empty = 4 * capacity
    out[...] = jnp.full(out.shape, -1.0, jnp.float32)
    out[:, 0:empty, :] = jnp.zeros((devices, empty, LANES), jnp.float32)

    def clear(i, carry):
        used[i] = 0
        return carry

    lax.fori_loop(0, devices, clear, 0)
    lane = lax.broadcasted_iota(jnp.int32, (1, LANES), 1)

    def place(i, carry):
        o = owner[i]
        j = used[o]
        used[o] = j + 1
        target[i] = o * capacity + j
        pair = offsets[i]
        out[o, pl.ds(j, 1), :] = pair[0:1]
        out[o, pl.ds(capacity + j, 1), :] = pair[1:2]
        out[o, pl.ds(2 * capacity + j, 1), :] = jnp.where(lane < count[i], charges[pl.ds(i, 1), :], 0.0)
        out[o, pl.ds(3 * capacity + j, 1), :] = cells[pl.ds(i, 1), :].astype(jnp.float32)
        out[o, pl.ds(4 * capacity + j, 1), :] = jnp.full((1, LANES), band[i], jnp.int32).astype(jnp.float32)
        return carry

    lax.fori_loop(0, owner.shape[0], place, 0)


def live_list(bands, live, capacity):
    total = bands.shape[0]

    def check(s, n):
        live[n] = s
        return n + jnp.where(bands[s] >= 0, 1, 0)

    return lax.fori_loop(0, total, check, jnp.int32(0))


def particle(recv, capacity, s):
    d = s // capacity
    j = s % capacity
    frac_x = recv[d, pl.ds(j, 1), :]
    frac_y = recv[d, pl.ds(capacity + j, 1), :]
    weight = recv[d, pl.ds(2 * capacity + j, 1), :]
    cell = recv[d, pl.ds(3 * capacity + j, 1), :].astype(jnp.int32)
    column = cell % NG
    after = (column + 1) % NG
    row = cell // NG
    left = (1.0 - frac_x).astype(jnp.bfloat16).astype(jnp.float32)
    right = frac_x.astype(jnp.bfloat16).astype(jnp.float32)
    return frac_y, weight, row, column, after, left, right


def dot3(a_high, a_low, b_high, b_low):
    dot = functools.partial(jnp.dot, preferred_element_type=jnp.float32)
    return dot(a_high, b_high) + (dot(a_high, b_low) + dot(a_low, b_high))


def split(values):
    high = values.astype(jnp.bfloat16)
    return high, (values - high.astype(jnp.float32)).astype(jnp.bfloat16)


def deposit_kernel(capacity, rows, bands, recv, table_high, table_low, lines, spectrum, edges, live, dens, hi, lo):
    total = bands.shape[0]
    n_live = live_list(bands, live, capacity)
    dens[...] = jnp.zeros(dens.shape, jnp.float32)
    sub8 = lax.broadcasted_iota(jnp.int32, (8, LANES), 0)
    sub_all = lax.broadcasted_iota(jnp.int32, (LANES, LANES), 0)

    def one(slot_at):
        alive = slot_at < n_live
        s = live[jnp.where(alive, slot_at, 0)]
        frac_y, weight, row, column, after, left, right = particle(recv, capacity, s)
        weight = jnp.where(alive, weight, 0.0)
        lower = (weight * (1.0 - frac_y)).astype(jnp.bfloat16).astype(jnp.float32)
        upper = (weight * frac_y).astype(jnp.bfloat16).astype(jnp.float32)
        main = jnp.where(row == sub8, lower, jnp.where(row + 1 == sub8, upper, 0.0))
        tail = jnp.where((sub8 == 0) & (row == 7), upper, 0.0)
        tall = jnp.concatenate([main, tail], axis=0)
        chunk = column // LANES
        chunk_after = after // LANES
        row_left = jnp.concatenate([jnp.where(chunk == a, tall, 0.0) for a in range(CHUNKS)], axis=0)
        row_right = jnp.concatenate([jnp.where(chunk_after == a, tall, 0.0) for a in range(CHUNKS)], axis=0)
        col_left = jnp.where(column % LANES == sub_all, left, 0.0)
        col_right = jnp.where(after % LANES == sub_all, right, 0.0)
        lhs = jnp.concatenate([row_left.astype(jnp.bfloat16), row_right.astype(jnp.bfloat16)], axis=1)
        rhs = jnp.concatenate([col_left.astype(jnp.bfloat16), col_right.astype(jnp.bfloat16)], axis=1)
        values = lax.dot_general(lhs, rhs, (((1,), (1,)), ((), ())), preferred_element_type=jnp.float32)
        return jnp.maximum(bands[s], 0), values

    def group(g, carry):
        results = [one(g * UNROLL + k) for k in range(UNROLL)]
        for band, values in results:
            start = pl.multiple_of(band * 8, 8)
            for a in range(CHUNKS):
                lanes = slice(a * LANES, (a + 1) * LANES)
                dens[pl.ds(start, 16), lanes] += values[a * 16 : (a + 1) * 16]
        return carry

    lax.fori_loop(0, (n_live + UNROLL - 1) // UNROLL, group, 0)
    high, low = split(dens[...])
    hi[...] = high
    lo[...] = low
    width = 256
    spill = []
    for n in range(NG // width):
        cols = slice(n * width, (n + 1) * width)
        values = dot3(hi[...], lo[...], table_high[:, cols], table_low[:, cols])
        spectrum[:, cols] = values[:rows]
        edges[2:3, cols] = values[rows : rows + 1]
    eight = lines[T_EIGHT * 8 : T_EIGHT * 8 + 8]
    tiles = rows // 8

    def fold(t, carry):
        fwd, bwd = carry
        fwd = eight * fwd + spectrum[pl.ds(pl.multiple_of(t * 8, 8), 8), :]
        bwd = eight * bwd + spectrum[pl.ds(pl.multiple_of((tiles - 1 - t) * 8, 8), 8), :]
        return fwd, bwd

    nothing = jnp.zeros((8, NG), jnp.float32)
    fwd, bwd = lax.fori_loop(0, tiles, fold, (nothing, nothing))
    edges[0:1] = jnp.sum(fwd * lines[T_FEND * 8 : T_FEND * 8 + 8], axis=0, keepdims=True)
    edges[1:2] = jnp.sum(bwd * lines[T_BEND * 8 : T_BEND * 8 + 8], axis=0, keepdims=True)
    edges[3:5] = spectrum[0:2]
    edges[5:6] = spectrum[rows - 1 : rows]
    edges[6:8] = jnp.zeros((2, NG), jnp.float32)


def solve_kernel(capacity, rows, bands, place, recv, spectrum, gathered, table_high, table_low, lines, potential, forces, live, wave, hi, lo, field):
    pens = gathered.shape[0]
    mine = place[0]

    def table(which):
        return lines[which * 8 : which * 8 + 8]

    def row_of(pen, which):
        return gathered[lax.rem(pen + 2 * pens, pens), which : which + 1]

    last_power = table(T_LAST)[0:1]
    before = jnp.zeros((1, NG), jnp.float32)
    beyond = jnp.zeros((1, NG), jnp.float32)
    for j in range(pens):
        lag = lines[T_LAG * 8 + j : T_LAG * 8 + j + 1]
        behind, ahead = mine - 1 - j, mine + 1 + j
        before += lag * (row_of(behind, 0) + last_power * row_of(behind - 1, 2))
        beyond += lag * (row_of(ahead, 1) + row_of(ahead - 1, 2))
    incoming = row_of(mine - 1, 2)
    next_zero = row_of(mine + 1, 3) + row_of(mine, 2)
    next_one = row_of(mine + 1, 4)
    last_before = row_of(mine - 1, 5)
    spectrum_first = spectrum[0:1] + incoming
    first_row = lax.broadcasted_iota(jnp.int32, (8, NG), 0) == 0
    tiles = rows // 8

    def tile_of(t):
        values = spectrum[pl.ds(pl.multiple_of(t * 8, 8), 8), :]
        return values + jnp.where(first_row & (t == 0), incoming, 0.0)

    def backward(i, carry):
        t = tiles - 1 - i
        x = tile_of(t)
        x = x + table(T_B1) * pltpu.roll(x, 7, 0)
        x = x + table(T_B2) * pltpu.roll(x, 6, 0)
        x = x + table(T_B4) * pltpu.roll(x, 4, 0)
        x = x + table(T_BC) * carry
        wave[pl.ds(pl.multiple_of(t * 8 + 8, 8), 8), :] = x
        return x[0:1]

    first_back = lax.fori_loop(0, tiles, backward, beyond)
    norm = table(T_NORM)[0:1]

    def forward(t, carry):
        d = tile_of(t)
        x = d + table(T_F1) * pltpu.roll(d, 1, 0)
        x = x + table(T_F2) * pltpu.roll(x, 2, 0)
        x = x + table(T_F4) * pltpu.roll(x, 4, 0)
        x = x + table(T_FC) * carry
        where = pl.ds(pl.multiple_of(t * 8 + 8, 8), 8)
        wave[where, :] = table(T_NORM) * (x + wave[where, :] - d)
        return x[7:8]

    final = lax.fori_loop(0, tiles, forward, before)
    diagonal = table(T_DIAG)[0:1]
    root = table(T_FC)[0:1]
    scale = 1.0 / NG
    up1 = norm * (before + root * first_back)
    up2 = diagonal * up1 - wave[8:9] - scale * last_before
    down0 = norm * (root * final + beyond)
    down1 = diagonal * down0 - wave[rows + 7 : rows + 8] - scale * next_zero
    down2 = diagonal * down1 - down0 - scale * next_one
    wave[0:6] = jnp.zeros((6, NG), jnp.float32)
    wave[6:7] = up2
    wave[7:8] = up1
    wave[rows + 8 : rows + 9] = down0
    wave[rows + 9 : rows + 10] = down1
    wave[rows + 10 : rows + 11] = down2
    wave[rows + 11 : rows + 16] = jnp.zeros((5, NG), jnp.float32)
    high, low = split(wave[...])
    hi[...] = high
    lo[...] = low
    width = 256
    for n in range(NG // width):
        cols = slice(n * width, (n + 1) * width)
        wave[:, cols] = dot3(hi[...], lo[...], table_high[:, cols], table_low[:, cols])
    potential[...] = wave[8 : rows + 8]

    def derive(t, carry):
        base = pl.multiple_of(t * 8, 8)
        tall = wave[pl.ds(base, 24), :] if False else jnp.concatenate(
            [
                wave[pl.ds(base, 8), :],
                wave[pl.ds(pl.multiple_of(base + 8, 8), 8), :],
                wave[pl.ds(pl.multiple_of(jnp.minimum(base + 16, rows + 8), 8), 8), :],
            ],
            axis=0,
        )
        middle = tall[8:16]
        along_x = (8.0 * (pltpu.roll(middle, NG - 1, 1) - pltpu.roll(middle, 1, 1))
                   - (pltpu.roll(middle, NG - 2, 1) - pltpu.roll(middle, 2, 1))) / -12.0
        along_y = (8.0 * (tall[9:17] - tall[7:15]) - (tall[10:18] - tall[6:14])) / -12.0

        @pl.when(t < tiles)
        def _():
            field[t, 0:8, :] = along_x
            field[t, 8:16, :] = along_y

        @pl.when(t > 0)
        def _():
            field[t - 1, 16:17, :] = along_x[0:1]
            field[t - 1, 17:18, :] = along_y[0:1]

        return carry

    lax.fori_loop(0, tiles + 1, derive, 0)
    for t in range(tiles):
        field[t, 18:24, :] = jnp.zeros((6, NG), jnp.float32)

    n_live = live_list(bands, live, capacity)
    forces[...] = jnp.zeros(forces.shape, jnp.float32)
    sub8 = lax.broadcasted_iota(jnp.int32, (8, LANES), 0)

    def pick(values, index):
        return jnp.take_along_axis(values, index, axis=1, mode="promise_in_bounds")

    def one(slot_at):
        s = live[jnp.minimum(slot_at, n_live - 1)]
        band = bands[s]
        frac_y, weight, row, column, after, left, right = particle(recv, capacity, s)
        index = jnp.broadcast_to(column % LANES, (8, LANES))
        index_after = jnp.broadcast_to(after % LANES, (8, LANES))
        chunk = jnp.broadcast_to(column // LANES, (8, LANES))
        chunk_after = jnp.broadcast_to(after // LANES, (8, LANES))
        mixed = []
        for part in range(3):
            near = jnp.zeros((8, LANES), jnp.float32)
            far = near
            for a in range(CHUNKS):
                values = field[band, part * 8 : part * 8 + 8, a * LANES : (a + 1) * LANES]
                near = jnp.where(chunk == a, pick(values, index), near)
                far = jnp.where(chunk_after == a, pick(values, index_after), far)
            mixed.append(left * near + right * far)
        row_weight = jnp.where(row == sub8, 1.0 - frac_y, jnp.where(row + 1 == sub8, frac_y, 0.0))
        edge = jnp.where(row == 7, frac_y, 0.0)
        out = [
            weight * (jnp.sum(row_weight * mixed[c], axis=0, keepdims=True) + edge * mixed[2][c : c + 1])
            for c in range(2)
        ]
        return s, jnp.concatenate(out, axis=0)

    def group(g, carry):
        results = [one(g * UNROLL + k) for k in range(UNROLL)]
        for s, values in results:
            forces[s] = values
        return carry

    lax.fori_loop(0, (n_live + UNROLL - 1) // UNROLL, group, 0)


def shards(block_owner, block_band, block_count, cells, offsets, charges):
    plane_count = lax.axis_size("pln")
    pen_count = lax.axis_size("pen")
    devices = plane_count * pen_count
    local_blocks, block_len = charges.shape
    capacity = max(2, 2 * local_blocks // devices)
    total = devices * capacity
    rows = NG // pen_count
    tall = round_up(5 * capacity, 8)
    smem = pl.BlockSpec(memory_space=pltpu.SMEM)
    vmem = pl.BlockSpec(memory_space=pltpu.VMEM)
    params = pltpu.CompilerParams(vmem_limit_bytes=VMEM_LIMIT)
    packed, target = pl.pallas_call(
        functools.partial(pack_kernel, capacity),
        out_shape=(
            jax.ShapeDtypeStruct((devices, tall, LANES), jnp.float32),
            jax.ShapeDtypeStruct((local_blocks,), jnp.int32),
        ),
        in_specs=[smem] * 3 + [vmem] * 3,
        out_specs=(vmem, smem),
        scratch_shapes=[pltpu.SMEM((devices,), jnp.int32)],
        compiler_params=params,
        name="pack",
    )(block_owner[:, 0], block_band, block_count, cells, offsets, charges)
    received = lax.all_to_all(packed, ("pln", "pen"), split_axis=0, concat_axis=0, tiled=True)
    bands = received[:, 4 * capacity : 5 * capacity, 0].reshape(total).astype(jnp.int32)
    table_high, table_low = (jnp.asarray(t) for t in hartley_tables())
    lines = jnp.asarray(line_tables(pen_count))
    spectrum, edges = pl.pallas_call(
        functools.partial(deposit_kernel, capacity, rows),
        out_shape=(
            jax.ShapeDtypeStruct((rows, NG), jnp.float32),
            jax.ShapeDtypeStruct((8, NG), jnp.float32),
        ),
        in_specs=[smem] + [vmem] * 4,
        out_specs=(vmem, vmem),
        scratch_shapes=[
            pltpu.SMEM((total + 8,), jnp.int32),
            pltpu.VMEM((rows + 8, NG), jnp.float32),
            pltpu.VMEM((rows + 8, NG), jnp.bfloat16),
            pltpu.VMEM((rows + 8, NG), jnp.bfloat16),
        ],
        compiler_params=params,
        name="deposit",
    )(bands, received, table_high, table_low, lines)
    gathered = lax.all_gather(edges, "pen", axis=0, tiled=False)
    place = lax.axis_index("pen").astype(jnp.int32).reshape(1)
    potential, slot_forces = pl.pallas_call(
        functools.partial(solve_kernel, capacity, rows),
        out_shape=(
            jax.ShapeDtypeStruct((rows, NG), jnp.float32),
            jax.ShapeDtypeStruct((total, 2, LANES), jnp.float32),
        ),
        in_specs=[smem] * 2 + [vmem] * 6,
        out_specs=(vmem, vmem),
        scratch_shapes=[
            pltpu.SMEM((total + 8,), jnp.int32),
            pltpu.VMEM((rows + 16, NG), jnp.float32),
            pltpu.VMEM((rows + 16, NG), jnp.bfloat16),
            pltpu.VMEM((rows + 16, NG), jnp.bfloat16),
            pltpu.VMEM((rows // 8, 24, NG), jnp.float32),
        ],
        compiler_params=params,
        name="solve",
    )(bands, place, received, spectrum, gathered, table_high, table_low, lines)
    returned = lax.all_to_all(
        slot_forces.reshape(devices, capacity, 2, block_len),
        ("pln", "pen"),
        split_axis=0,
        concat_axis=0,
        tiled=True,
    )
    forces = returned.reshape(total, 2, block_len)[target]
    return (potential[None], forces)


def solution(mesh):
    placed = (
        P(("pln", "pen"), None),
        P(("pln", "pen")),
        P(("pln", "pen")),
        P(("pln", "pen"), None),
        P(("pln", "pen"), None, None),
        P(("pln", "pen"), None),
    )
    return jax.shard_map(
        shards,
        mesh=mesh,
        in_specs=placed,
        out_specs=(P("pln", "pen", None), P(("pln", "pen"), None, None)),
        check_vma=False,
    )
```

```python
import functools
import math

import jax
import jax.numpy as jnp
import numpy as np
from jax import lax
from jax.experimental import pallas as pl
from jax.experimental.pallas import tpu as pltpu
from jax.sharding import PartitionSpec as P

NG = 1024
LANES = 128
CHUNKS = NG // LANES
screening = 2e-05
VMEM_LIMIT = 48 * 1024 * 1024
UNROLL = 4


def round_up(value, step):
    return -(-value // step) * step


@functools.lru_cache(None)
def hartley_tables():
    index = np.arange(NG)
    angle = 2.0 * np.pi / NG * (index[:, None] * index[None, :] % NG)
    table = np.cos(angle) + np.sin(angle)
    high = table.astype(jnp.bfloat16)
    low = (table - high.astype(np.float64)).astype(jnp.bfloat16)
    return high, low


@functools.lru_cache(None)
def line_tables(pen_count):
    rows = NG // pen_count
    shift = 4.0 * np.sin(np.pi * np.arange(NG) / NG) ** 2 + screening
    root = 1.0 + shift / 2.0 - np.sqrt(shift + shift * shift / 4.0)
    i = np.arange(8)[:, None]

    def power(exponent):
        return root[None, :] ** (exponent + np.zeros((8, 1)))

    tiles = [
        power(7 - i),
        power(i),
        power(8),
        np.where(i >= 1, power(1), 0.0),
        np.where(i >= 2, power(2), 0.0),
        np.where(i >= 4, power(4), 0.0),
        np.where(i <= 6, power(1), 0.0),
        np.where(i <= 5, power(2), 0.0),
        np.where(i <= 3, power(4), 0.0),
        power(i + 1),
        power(8 - i),
        np.broadcast_to(1.0 / ((1.0 / root - root) * NG), (8, NG)),
        np.broadcast_to(2.0 + shift, (8, NG)),
        power(rows - 1),
    ]
    lags = np.arange(round_up(pen_count, 8))[:, None]
    tiles.append(root[None, :] ** (lags * rows) / (1.0 - root[None, :] ** NG))
    return np.concatenate(tiles, axis=0).astype(np.float32)


T_FEND, T_BEND, T_EIGHT, T_F1, T_F2, T_F4, T_B1, T_B2, T_B4, T_FC, T_BC, T_NORM, T_DIAG, T_LAST, T_LAG = range(15)


def fetch(sources, targets, sems):
    copies = [pltpu.make_async_copy(a, b, sems.at[i]) for i, (a, b) in enumerate(zip(sources, targets))]
    for copy in copies:
        copy.start()
    return copies


def pack_kernel(capacity, owner_h, band_h, count_h, cells_h, offsets_h, charges_h, out, target,
                owner, band, count, cells, offsets, charges, used, sems):
    devices = out.shape[0]
    copies = fetch(
        (owner_h, band_h, count_h, cells_h, offsets_h, charges_h),
        (owner, band, count, cells, offsets, charges),
        sems,
    )
    empty = 4 * capacity
    out[...] = jnp.full(out.shape, -1.0, jnp.float32)
    out[:, 0:empty, :] = jnp.zeros((devices, empty, LANES), jnp.float32)

    def clear(i, carry):
        used[i] = 0
        return carry

    lax.fori_loop(0, devices, clear, 0)
    lane = lax.broadcasted_iota(jnp.int32, (1, LANES), 1)
    for copy in copies:
        copy.wait()

    def place(i, carry):
        o = owner[i]
        j = used[o]
        used[o] = j + 1
        target[i] = o * capacity + j
        pair = offsets[i]
        out[o, pl.ds(j, 1), :] = pair[0:1]
        out[o, pl.ds(capacity + j, 1), :] = pair[1:2]
        out[o, pl.ds(2 * capacity + j, 1), :] = jnp.where(lane < count[i], charges[pl.ds(i, 1), :], 0.0)
        out[o, pl.ds(3 * capacity + j, 1), :] = cells[pl.ds(i, 1), :].astype(jnp.float32)
        out[o, pl.ds(4 * capacity + j, 1), :] = jnp.full((1, LANES), band[i], jnp.int32).astype(jnp.float32)
        return carry

    lax.fori_loop(0, owner.shape[0], place, 0)


def peer(index, pens):
    return (lax.div(index, pens), lax.rem(index, pens))


def exchange_kernel(planes, pens, source, target, send_sems, recv_sems, own_sem):
    count = planes * pens
    me = lax.axis_index("pln") * pens + lax.axis_index("pen")
    barrier = pltpu.get_barrier_semaphore()

    def greet(k, carry):
        other = peer(lax.rem(me + k, count), pens)
        pl.semaphore_signal(barrier, inc=1, device_id=other, device_id_type=pl.DeviceIdType.MESH)
        return carry

    own = pltpu.make_async_copy(source.at[me], target.at[me], own_sem)
    own.start()
    lax.fori_loop(1, count, greet, 0)
    pl.semaphore_wait(barrier, count - 1)

    def copy_to(k):
        to = lax.rem(me + k, count)
        return pltpu.make_async_remote_copy(
            src_ref=source.at[to],
            dst_ref=target.at[me],
            send_sem=send_sems.at[k],
            recv_sem=recv_sems.at[k],
            device_id=peer(to, pens),
            device_id_type=pl.DeviceIdType.MESH,
        )

    def send(k, carry):
        copy_to(k).start()
        return carry

    def finish(k, carry):
        copy_to(k).wait_send()
        pltpu.make_async_remote_copy(
            src_ref=source.at[me],
            dst_ref=target.at[lax.rem(me - k + count, count)],
            send_sem=send_sems.at[k],
            recv_sem=recv_sems.at[k],
            device_id=peer(lax.rem(me - k + count, count), pens),
            device_id_type=pl.DeviceIdType.MESH,
        ).wait_recv()
        return carry

    lax.fori_loop(1, count, send, 0)
    lax.fori_loop(1, count, finish, 0)
    own.wait()


def exchange(values, planes, pens, number):
    place = pl.BlockSpec(memory_space=pl.ANY)
    return pl.pallas_call(
        functools.partial(exchange_kernel, planes, pens),
        out_shape=jax.ShapeDtypeStruct(values.shape, values.dtype),
        in_specs=[place],
        out_specs=place,
        scratch_shapes=[
            pltpu.SemaphoreType.DMA((planes * pens,)),
            pltpu.SemaphoreType.DMA((planes * pens,)),
            pltpu.SemaphoreType.DMA,
        ],
        compiler_params=pltpu.CompilerParams(collective_id=number, has_side_effects=True),
        name="exchange",
    )(values)


def share_kernel(pens, source, target, send_sems, recv_sems, own_sem):
    mine = lax.axis_index("pen")
    plane = lax.axis_index("pln")
    barrier = pltpu.get_barrier_semaphore()
    own = pltpu.make_async_copy(source, target.at[mine], own_sem)
    own.start()
    for k in range(1, pens):
        other = (plane, lax.rem(mine + k, pens))
        pl.semaphore_signal(barrier, inc=1, device_id=other, device_id_type=pl.DeviceIdType.MESH)
    pl.semaphore_wait(barrier, pens - 1)
    sends = []
    for k in range(1, pens):
        copy = pltpu.make_async_remote_copy(
            src_ref=source,
            dst_ref=target.at[mine],
            send_sem=send_sems.at[k],
            recv_sem=recv_sems.at[k],
            device_id=(plane, lax.rem(mine + k, pens)),
            device_id_type=pl.DeviceIdType.MESH,
        )
        copy.start()
        sends.append(copy)
    for k in range(1, pens):
        sends[k - 1].wait_send()
        behind = lax.rem(mine - k + pens, pens)
        pltpu.make_async_remote_copy(
            src_ref=source,
            dst_ref=target.at[behind],
            send_sem=send_sems.at[k],
            recv_sem=recv_sems.at[k],
            device_id=(plane, behind),
            device_id_type=pl.DeviceIdType.MESH,
        ).wait_recv()
    own.wait()


def share(values, pens, number):
    place = pl.BlockSpec(memory_space=pltpu.VMEM)
    return pl.pallas_call(
        functools.partial(share_kernel, pens),
        out_shape=jax.ShapeDtypeStruct((pens,) + values.shape, values.dtype),
        in_specs=[place],
        out_specs=place,
        scratch_shapes=[
            pltpu.SemaphoreType.DMA((pens,)),
            pltpu.SemaphoreType.DMA((pens,)),
            pltpu.SemaphoreType.DMA,
        ],
        compiler_params=pltpu.CompilerParams(collective_id=number, has_side_effects=True),
        name="share",
    )(values)


def live_list(bands, live, capacity):
    total = bands.shape[0]

    def check(s, n):
        live[n] = s
        return n + jnp.where(bands[s] >= 0, 1, 0)

    return lax.fori_loop(0, total, check, jnp.int32(0))


def particle(recv, capacity, s):
    d = s // capacity
    j = s % capacity
    frac_x = recv[d, pl.ds(j, 1), :]
    frac_y = recv[d, pl.ds(capacity + j, 1), :]
    weight = recv[d, pl.ds(2 * capacity + j, 1), :]
    cell = recv[d, pl.ds(3 * capacity + j, 1), :].astype(jnp.int32)
    column = cell % NG
    after = (column + 1) % NG
    row = cell // NG
    left = (1.0 - frac_x).astype(jnp.bfloat16).astype(jnp.float32)
    right = frac_x.astype(jnp.bfloat16).astype(jnp.float32)
    return frac_y, weight, row, column, after, left, right


def dot3(a_high, a_low, b_high, b_low):
    dot = functools.partial(jnp.dot, preferred_element_type=jnp.float32)
    return dot(a_high, b_high) + (dot(a_high, b_low) + dot(a_low, b_high))


def split(values):
    high = values.astype(jnp.bfloat16)
    return high, (values - high.astype(jnp.float32)).astype(jnp.bfloat16)


def deposit_kernel(capacity, rows, bands, recv, table_high_h, table_low_h, lines_h, spectrum, edges,
                   live, dens, hi, lo, table_high, table_low, lines, sems):
    total = bands.shape[0]
    copies = fetch((table_high_h, table_low_h, lines_h), (table_high, table_low, lines), sems)
    n_live = live_list(bands, live, capacity)
    dens[...] = jnp.zeros(dens.shape, jnp.float32)
    sub8 = lax.broadcasted_iota(jnp.int32, (8, LANES), 0)
    sub_all = lax.broadcasted_iota(jnp.int32, (LANES, LANES), 0)

    def one(slot_at):
        alive = slot_at < n_live
        s = live[jnp.where(alive, slot_at, 0)]
        frac_y, weight, row, column, after, left, right = particle(recv, capacity, s)
        weight = jnp.where(alive, weight, 0.0)
        lower = (weight * (1.0 - frac_y)).astype(jnp.bfloat16).astype(jnp.float32)
        upper = (weight * frac_y).astype(jnp.bfloat16).astype(jnp.float32)
        main = jnp.where(row == sub8, lower, jnp.where(row + 1 == sub8, upper, 0.0))
        tail = jnp.where((sub8 == 0) & (row == 7), upper, 0.0)
        tall = jnp.concatenate([main, tail], axis=0)
        chunk = column // LANES
        chunk_after = after // LANES
        row_left = jnp.concatenate([jnp.where(chunk == a, tall, 0.0) for a in range(CHUNKS)], axis=0)
        row_right = jnp.concatenate([jnp.where(chunk_after == a, tall, 0.0) for a in range(CHUNKS)], axis=0)
        col_left = jnp.where(column % LANES == sub_all, left, 0.0)
        col_right = jnp.where(after % LANES == sub_all, right, 0.0)
        lhs = jnp.concatenate([row_left.astype(jnp.bfloat16), row_right.astype(jnp.bfloat16)], axis=1)
        rhs = jnp.concatenate([col_left.astype(jnp.bfloat16), col_right.astype(jnp.bfloat16)], axis=1)
        values = lax.dot_general(lhs, rhs, (((1,), (1,)), ((), ())), preferred_element_type=jnp.float32)
        return jnp.maximum(bands[s], 0), values

    def group(g, carry):
        results = [one(g * UNROLL + k) for k in range(UNROLL)]
        for band, values in results:
            start = pl.multiple_of(band * 8, 8)
            for a in range(CHUNKS):
                lanes = slice(a * LANES, (a + 1) * LANES)
                dens[pl.ds(start, 16), lanes] += values[a * 16 : (a + 1) * 16]
        return carry

    lax.fori_loop(0, (n_live + UNROLL - 1) // UNROLL, group, 0)
    high, low = split(dens[...])
    hi[...] = high
    lo[...] = low
    width = 256
    for copy in copies:
        copy.wait()
    for n in range(NG // width):
        cols = slice(n * width, (n + 1) * width)
        values = dot3(hi[...], lo[...], table_high[:, cols], table_low[:, cols])
        spectrum[:, cols] = values[:rows]
        edges[2:3, cols] = values[rows : rows + 1]
    eight = lines[T_EIGHT * 8 : T_EIGHT * 8 + 8]
    tiles = rows // 8

    def fold(t, carry):
        fwd, bwd = carry
        fwd = eight * fwd + spectrum[pl.ds(pl.multiple_of(t * 8, 8), 8), :]
        bwd = eight * bwd + spectrum[pl.ds(pl.multiple_of((tiles - 1 - t) * 8, 8), 8), :]
        return fwd, bwd

    nothing = jnp.zeros((8, NG), jnp.float32)
    fwd, bwd = lax.fori_loop(0, tiles, fold, (nothing, nothing))
    edges[0:1] = jnp.sum(fwd * lines[T_FEND * 8 : T_FEND * 8 + 8], axis=0, keepdims=True)
    edges[1:2] = jnp.sum(bwd * lines[T_BEND * 8 : T_BEND * 8 + 8], axis=0, keepdims=True)
    edges[3:5] = spectrum[0:2]
    edges[5:6] = spectrum[rows - 1 : rows]
    edges[6:8] = jnp.zeros((2, NG), jnp.float32)


def solve_kernel(capacity, rows, bands, place, recv, spectrum, gathered, table_high_h, table_low_h, lines_h, potential, forces,
                 live, wave, hi, lo, field, table_high, table_low, lines, sems):
    copies = fetch((lines_h, table_high_h, table_low_h), (lines, table_high, table_low), sems)
    copies[0].wait()
    pens = gathered.shape[0]
    mine = place[0]

    def table(which):
        return lines[which * 8 : which * 8 + 8]

    def row_of(pen, which):
        return gathered[lax.rem(pen + 2 * pens, pens), which : which + 1]

    last_power = table(T_LAST)[0:1]
    before = jnp.zeros((1, NG), jnp.float32)
    beyond = jnp.zeros((1, NG), jnp.float32)
    for j in range(pens):
        lag = lines[T_LAG * 8 + j : T_LAG * 8 + j + 1]
        behind, ahead = mine - 1 - j, mine + 1 + j
        before += lag * (row_of(behind, 0) + last_power * row_of(behind - 1, 2))
        beyond += lag * (row_of(ahead, 1) + row_of(ahead - 1, 2))
    incoming = row_of(mine - 1, 2)
    next_zero = row_of(mine + 1, 3) + row_of(mine, 2)
    next_one = row_of(mine + 1, 4)
    last_before = row_of(mine - 1, 5)
    spectrum_first = spectrum[0:1] + incoming
    first_row = lax.broadcasted_iota(jnp.int32, (8, NG), 0) == 0
    tiles = rows // 8

    def tile_of(t):
        values = spectrum[pl.ds(pl.multiple_of(t * 8, 8), 8), :]
        return values + jnp.where(first_row & (t == 0), incoming, 0.0)

    def backward(i, carry):
        t = tiles - 1 - i
        x = tile_of(t)
        x = x + table(T_B1) * pltpu.roll(x, 7, 0)
        x = x + table(T_B2) * pltpu.roll(x, 6, 0)
        x = x + table(T_B4) * pltpu.roll(x, 4, 0)
        x = x + table(T_BC) * carry
        wave[pl.ds(pl.multiple_of(t * 8 + 8, 8), 8), :] = x
        return x[0:1]

    first_back = lax.fori_loop(0, tiles, backward, beyond)
    norm = table(T_NORM)[0:1]

    def forward(t, carry):
        d = tile_of(t)
        x = d + table(T_F1) * pltpu.roll(d, 1, 0)
        x = x + table(T_F2) * pltpu.roll(x, 2, 0)
        x = x + table(T_F4) * pltpu.roll(x, 4, 0)
        x = x + table(T_FC) * carry
        where = pl.ds(pl.multiple_of(t * 8 + 8, 8), 8)
        wave[where, :] = table(T_NORM) * (x + wave[where, :] - d)
        return x[7:8]

    final = lax.fori_loop(0, tiles, forward, before)
    diagonal = table(T_DIAG)[0:1]
    root = table(T_FC)[0:1]
    scale = 1.0 / NG
    up1 = norm * (before + root * first_back)
    up2 = diagonal * up1 - wave[8:9] - scale * last_before
    down0 = norm * (root * final + beyond)
    down1 = diagonal * down0 - wave[rows + 7 : rows + 8] - scale * next_zero
    down2 = diagonal * down1 - down0 - scale * next_one
    wave[0:6] = jnp.zeros((6, NG), jnp.float32)
    wave[6:7] = up2
    wave[7:8] = up1
    wave[rows + 8 : rows + 9] = down0
    wave[rows + 9 : rows + 10] = down1
    wave[rows + 10 : rows + 11] = down2
    wave[rows + 11 : rows + 16] = jnp.zeros((5, NG), jnp.float32)
    high, low = split(wave[...])
    hi[...] = high
    lo[...] = low
    width = 256
    copies[1].wait()
    copies[2].wait()
    for n in range(NG // width):
        cols = slice(n * width, (n + 1) * width)
        wave[:, cols] = dot3(hi[...], lo[...], table_high[:, cols], table_low[:, cols])
    potential[...] = wave[8 : rows + 8]

    def derive(t, carry):
        base = pl.multiple_of(t * 8, 8)
        tall = jnp.concatenate(
            [
                wave[pl.ds(base, 8), :],
                wave[pl.ds(pl.multiple_of(base + 8, 8), 8), :],
                wave[pl.ds(pl.multiple_of(jnp.minimum(base + 16, rows + 8), 8), 8), :],
            ],
            axis=0,
        )
        middle = tall[8:16]
        along_x = (8.0 * (pltpu.roll(middle, NG - 1, 1) - pltpu.roll(middle, 1, 1))
                   - (pltpu.roll(middle, NG - 2, 1) - pltpu.roll(middle, 2, 1))) / -12.0
        along_y = (8.0 * (tall[9:17] - tall[7:15]) - (tall[10:18] - tall[6:14])) / -12.0

        @pl.when(t < tiles)
        def _():
            field[t, 0:8, :] = along_x
            field[t, 8:16, :] = along_y

        @pl.when(t > 0)
        def _():
            field[t - 1, 16:17, :] = along_x[0:1]
            field[t - 1, 17:18, :] = along_y[0:1]

        return carry

    lax.fori_loop(0, tiles + 1, derive, 0)
    for t in range(tiles):
        field[t, 18:24, :] = jnp.zeros((6, NG), jnp.float32)

    n_live = live_list(bands, live, capacity)
    forces[...] = jnp.zeros(forces.shape, jnp.float32)
    sub8 = lax.broadcasted_iota(jnp.int32, (8, LANES), 0)

    def pick(values, index):
        return jnp.take_along_axis(values, index, axis=1, mode="promise_in_bounds")

    def one(slot_at):
        s = live[jnp.minimum(slot_at, n_live - 1)]
        band = bands[s]
        frac_y, weight, row, column, after, left, right = particle(recv, capacity, s)
        index = jnp.broadcast_to(column % LANES, (8, LANES))
        index_after = jnp.broadcast_to(after % LANES, (8, LANES))
        chunk = jnp.broadcast_to(column // LANES, (8, LANES))
        chunk_after = jnp.broadcast_to(after // LANES, (8, LANES))
        mixed = []
        for part in range(3):
            near = jnp.zeros((8, LANES), jnp.float32)
            far = near
            for a in range(CHUNKS):
                values = field[band, part * 8 : part * 8 + 8, a * LANES : (a + 1) * LANES]
                near = jnp.where(chunk == a, pick(values, index), near)
                far = jnp.where(chunk_after == a, pick(values, index_after), far)
            mixed.append(left * near + right * far)
        row_weight = jnp.where(row == sub8, 1.0 - frac_y, jnp.where(row + 1 == sub8, frac_y, 0.0))
        edge = jnp.where(row == 7, frac_y, 0.0)
        out = [
            weight * (jnp.sum(row_weight * mixed[c], axis=0, keepdims=True) + edge * mixed[2][c : c + 1])
            for c in range(2)
        ]
        return s, out

    def group(g, carry):
        results = [one(g * UNROLL + k) for k in range(UNROLL)]
        for s, values in results:
            d = s // capacity
            j = s % capacity
            forces[d, pl.ds(j, 1), :] = values[0]
            forces[d, pl.ds(capacity + j, 1), :] = values[1]
        return carry

    lax.fori_loop(0, (n_live + UNROLL - 1) // UNROLL, group, 0)


def unpack_kernel(capacity, target, returned, out):
    def take(i, carry):
        d = target[i] // capacity
        j = target[i] % capacity
        out[i, 0:1, :] = returned[d, pl.ds(j, 1), :]
        out[i, 1:2, :] = returned[d, pl.ds(capacity + j, 1), :]
        return carry

    lax.fori_loop(0, out.shape[0], take, 0, unroll=4)


def shards(block_owner, block_band, block_count, cells, offsets, charges):
    plane_count = lax.axis_size("pln")
    pen_count = lax.axis_size("pen")
    devices = plane_count * pen_count
    local_blocks, block_len = charges.shape
    capacity = max(2, 2 * local_blocks // devices)
    total = devices * capacity
    rows = NG // pen_count
    tall = round_up(5 * capacity, 8)
    tall_back = round_up(2 * capacity, 8)
    smem = pl.BlockSpec(memory_space=pltpu.SMEM)
    vmem = pl.BlockSpec(memory_space=pltpu.VMEM)
    far = pl.BlockSpec(memory_space=pltpu.HBM)
    params = pltpu.CompilerParams(vmem_limit_bytes=VMEM_LIMIT)
    packed, target = pl.pallas_call(
        functools.partial(pack_kernel, capacity),
        out_shape=(
            jax.ShapeDtypeStruct((devices, tall, LANES), jnp.float32),
            jax.ShapeDtypeStruct((local_blocks,), jnp.int32),
        ),
        in_specs=[far] * 6,
        out_specs=(vmem, smem),
        scratch_shapes=[pltpu.SMEM((local_blocks,), jnp.int32)] * 3
        + [
            pltpu.VMEM(cells.shape, jnp.int32),
            pltpu.VMEM(offsets.shape, jnp.float32),
            pltpu.VMEM(charges.shape, jnp.float32),
            pltpu.SMEM((devices,), jnp.int32),
            pltpu.SemaphoreType.DMA((6,)),
        ],
        compiler_params=params,
        name="pack",
    )(block_owner[:, 0], block_band, block_count, cells, offsets, charges)
    received = exchange(packed, plane_count, pen_count, 0)
    bands = received[:, 4 * capacity : 5 * capacity, 0].reshape(total).astype(jnp.int32)
    table_high, table_low = (jnp.asarray(t) for t in hartley_tables())
    lines = jnp.asarray(line_tables(pen_count))
    table_scratch = [
        pltpu.VMEM((NG, NG), jnp.bfloat16),
        pltpu.VMEM((NG, NG), jnp.bfloat16),
        pltpu.VMEM(lines.shape, jnp.float32),
        pltpu.SemaphoreType.DMA((3,)),
    ]
    spectrum, edges = pl.pallas_call(
        functools.partial(deposit_kernel, capacity, rows),
        out_shape=(
            jax.ShapeDtypeStruct((rows, NG), jnp.float32),
            jax.ShapeDtypeStruct((8, NG), jnp.float32),
        ),
        in_specs=[smem, vmem] + [far] * 3,
        out_specs=(vmem, vmem),
        scratch_shapes=[
            pltpu.SMEM((total + 8,), jnp.int32),
            pltpu.VMEM((rows + 8, NG), jnp.float32),
            pltpu.VMEM((rows + 8, NG), jnp.bfloat16),
            pltpu.VMEM((rows + 8, NG), jnp.bfloat16),
        ]
        + table_scratch,
        compiler_params=params,
        name="deposit",
    )(bands, received, table_high, table_low, lines)
    gathered = share(edges, pen_count, 1)
    place = lax.axis_index("pen").astype(jnp.int32).reshape(1)
    potential, slot_forces = pl.pallas_call(
        functools.partial(solve_kernel, capacity, rows),
        out_shape=(
            jax.ShapeDtypeStruct((rows, NG), jnp.float32),
            jax.ShapeDtypeStruct((devices, tall_back, LANES), jnp.float32),
        ),
        in_specs=[smem] * 2 + [vmem] * 3 + [far] * 3,
        out_specs=(vmem, vmem),
        scratch_shapes=[
            pltpu.SMEM((total + 8,), jnp.int32),
            pltpu.VMEM((rows + 16, NG), jnp.float32),
            pltpu.VMEM((rows + 16, NG), jnp.bfloat16),
            pltpu.VMEM((rows + 16, NG), jnp.bfloat16),
            pltpu.VMEM((rows // 8, 24, NG), jnp.float32),
        ]
        + table_scratch,
        compiler_params=params,
        name="solve",
    )(bands, place, received, spectrum, gathered, table_high, table_low, lines)
    returned = exchange(slot_forces, plane_count, pen_count, 2)
    forces = pl.pallas_call(
        functools.partial(unpack_kernel, capacity),
        out_shape=jax.ShapeDtypeStruct((local_blocks, 2, block_len), jnp.float32),
        in_specs=[smem, vmem],
        out_specs=vmem,
        compiler_params=params,
        name="unpack",
    )(target, returned)
    return (potential[None], forces)


def solution(mesh):
    placed = (
        P(("pln", "pen"), None),
        P(("pln", "pen")),
        P(("pln", "pen")),
        P(("pln", "pen"), None),
        P(("pln", "pen"), None, None),
        P(("pln", "pen"), None),
    )
    return jax.shard_map(
        shards,
        mesh=mesh,
        in_specs=placed,
        out_specs=(P("pln", "pen", None), P(("pln", "pen"), None, None)),
        check_vma=False,
    )
```

```python
import functools
import math

import jax
import jax.numpy as jnp
import numpy as np
from jax import lax
from jax.experimental import pallas as pl
from jax.experimental.pallas import tpu as pltpu
from jax.sharding import PartitionSpec as P

NG = 1024
LANES = 128
CHUNKS = NG // LANES
screening = 2e-05
VMEM_LIMIT = 62 * 1024 * 1024
UNROLL = 4


def round_up(value, step):
    return -(-value // step) * step


@functools.lru_cache(None)
def hartley_tables():
    index = np.arange(NG)
    angle = 2.0 * np.pi / NG * (index[:, None] * index[None, :] % NG)
    table = np.cos(angle) + np.sin(angle)
    high = table.astype(jnp.bfloat16)
    low = (table - high.astype(np.float64)).astype(jnp.bfloat16)
    return high, low


@functools.lru_cache(None)
def line_tables(pen_count):
    rows = NG // pen_count
    shift = 4.0 * np.sin(np.pi * np.arange(NG) / NG) ** 2 + screening
    root = 1.0 + shift / 2.0 - np.sqrt(shift + shift * shift / 4.0)
    i = np.arange(8)[:, None]

    def power(exponent):
        return root[None, :] ** (exponent + np.zeros((8, 1)))

    tiles = [
        power(7 - i),
        power(i),
        power(8),
        np.where(i >= 1, power(1), 0.0),
        np.where(i >= 2, power(2), 0.0),
        np.where(i >= 4, power(4), 0.0),
        np.where(i <= 6, power(1), 0.0),
        np.where(i <= 5, power(2), 0.0),
        np.where(i <= 3, power(4), 0.0),
        power(i + 1),
        power(8 - i),
        np.broadcast_to(1.0 / ((1.0 / root - root) * NG), (8, NG)),
        np.broadcast_to(2.0 + shift, (8, NG)),
        power(rows - 1),
    ]
    lags = np.arange(round_up(pen_count, 8))[:, None]
    tiles.append(root[None, :] ** (lags * rows) / (1.0 - root[None, :] ** NG))
    return np.concatenate(tiles, axis=0).astype(np.float32)


T_FEND, T_BEND, T_EIGHT, T_F1, T_F2, T_F4, T_B1, T_B2, T_B4, T_FC, T_BC, T_NORM, T_DIAG, T_LAST, T_LAG = range(15)


def fetch(sources, targets, sems):
    copies = [pltpu.make_async_copy(a, b, sems.at[i]) for i, (a, b) in enumerate(zip(sources, targets))]
    for copy in copies:
        copy.start()
    return copies


def pack_kernel(capacity, owner_h, band_h, count_h, cells_h, offsets_h, charges_h, out, header, target,
                owner, band, count, cells, offsets, charges, used, sems):
    devices = out.shape[0]
    copies = fetch(
        (owner_h, band_h, count_h, cells_h, offsets_h, charges_h),
        (owner, band, count, cells, offsets, charges),
        sems,
    )
    out[...] = jnp.zeros(out.shape, jnp.float32)
    header[...] = jnp.full(header.shape, -1, jnp.int32)

    def clear(i, carry):
        used[i] = 0
        return carry

    lax.fori_loop(0, devices, clear, 0)
    lane = lax.broadcasted_iota(jnp.int32, (1, LANES), 1)
    for copy in copies:
        copy.wait()

    def place(i, carry):
        o = owner[i]
        j = used[o]
        used[o] = j + 1
        target[i] = o * capacity + j
        pair = offsets[i]
        out[o, pl.ds(j, 1), :] = pair[0:1]
        out[o, pl.ds(capacity + j, 1), :] = pair[1:2]
        out[o, pl.ds(2 * capacity + j, 1), :] = jnp.where(lane < count[i], charges[pl.ds(i, 1), :], 0.0)
        out[o, pl.ds(3 * capacity + j, 1), :] = cells[pl.ds(i, 1), :].astype(jnp.float32)
        header[o] = jnp.where(lane == j, band[i], header[o])
        return carry

    lax.fori_loop(0, owner.shape[0], place, 0)


def peer(index, pens):
    return (lax.div(index, pens), lax.rem(index, pens))


def exchange_kernel(planes, pens, arrays, *refs):
    sources, targets = refs[:arrays], refs[arrays : 2 * arrays]
    send_sems, recv_sems, own_sems = refs[2 * arrays :]
    count = planes * pens
    me = lax.axis_index("pln") * pens + lax.axis_index("pen")
    barrier = pltpu.get_barrier_semaphore()

    def greet(k, carry):
        other = peer(lax.rem(me + k, count), pens)
        pl.semaphore_signal(barrier, inc=1, device_id=other, device_id_type=pl.DeviceIdType.MESH)
        return carry

    own = [
        pltpu.make_async_copy(sources[n].at[me], targets[n].at[me], own_sems.at[n]) for n in range(arrays)
    ]
    for copy in own:
        copy.start()
    lax.fori_loop(1, count, greet, 0)
    pl.semaphore_wait(barrier, count - 1)

    def copy_of(n, k, source, target, other):
        return pltpu.make_async_remote_copy(
            src_ref=sources[n].at[source],
            dst_ref=targets[n].at[target],
            send_sem=send_sems.at[n, k],
            recv_sem=recv_sems.at[n, k],
            device_id=peer(other, pens),
            device_id_type=pl.DeviceIdType.MESH,
        )

    def send(k, carry):
        to = lax.rem(me + k, count)
        for n in range(arrays):
            copy_of(n, k, to, me, to).start()
        return carry

    def finish(k, carry):
        to = lax.rem(me + k, count)
        behind = lax.rem(me - k + count, count)
        for n in range(arrays):
            copy_of(n, k, to, me, to).wait_send()
            copy_of(n, k, me, behind, behind).wait_recv()
        return carry

    lax.fori_loop(1, count, send, 0)
    lax.fori_loop(1, count, finish, 0)
    for copy in own:
        copy.wait()


def exchange(values, planes, pens, number):
    place = pl.BlockSpec(memory_space=pl.ANY)
    arrays = len(values)
    return pl.pallas_call(
        functools.partial(exchange_kernel, planes, pens, arrays),
        out_shape=tuple(jax.ShapeDtypeStruct(v.shape, v.dtype) for v in values),
        in_specs=[place] * arrays,
        out_specs=(place,) * arrays,
        scratch_shapes=[
            pltpu.SemaphoreType.DMA((arrays, planes * pens)),
            pltpu.SemaphoreType.DMA((arrays, planes * pens)),
            pltpu.SemaphoreType.DMA((arrays,)),
        ],
        compiler_params=pltpu.CompilerParams(
            collective_id=number, has_side_effects=True, vmem_limit_bytes=VMEM_LIMIT
        ),
        name="exchange",
    )(*values)


def share_kernel(pens, source, target, send_sems, recv_sems, own_sem):
    mine = lax.axis_index("pen")
    plane = lax.axis_index("pln")
    barrier = pltpu.get_barrier_semaphore()
    own = pltpu.make_async_copy(source, target.at[mine], own_sem)
    own.start()
    for k in range(1, pens):
        other = (plane, lax.rem(mine + k, pens))
        pl.semaphore_signal(barrier, inc=1, device_id=other, device_id_type=pl.DeviceIdType.MESH)
    pl.semaphore_wait(barrier, pens - 1)
    sends = []
    for k in range(1, pens):
        copy = pltpu.make_async_remote_copy(
            src_ref=source,
            dst_ref=target.at[mine],
            send_sem=send_sems.at[k],
            recv_sem=recv_sems.at[k],
            device_id=(plane, lax.rem(mine + k, pens)),
            device_id_type=pl.DeviceIdType.MESH,
        )
        copy.start()
        sends.append(copy)
    for k in range(1, pens):
        sends[k - 1].wait_send()
        behind = lax.rem(mine - k + pens, pens)
        pltpu.make_async_remote_copy(
            src_ref=source,
            dst_ref=target.at[behind],
            send_sem=send_sems.at[k],
            recv_sem=recv_sems.at[k],
            device_id=(plane, behind),
            device_id_type=pl.DeviceIdType.MESH,
        ).wait_recv()
    own.wait()


def share(values, pens, number):
    place = pl.BlockSpec(memory_space=pltpu.VMEM)
    return pl.pallas_call(
        functools.partial(share_kernel, pens),
        out_shape=jax.ShapeDtypeStruct((pens,) + values.shape, values.dtype),
        in_specs=[place],
        out_specs=place,
        scratch_shapes=[
            pltpu.SemaphoreType.DMA((pens,)),
            pltpu.SemaphoreType.DMA((pens,)),
            pltpu.SemaphoreType.DMA,
        ],
        compiler_params=pltpu.CompilerParams(collective_id=number, has_side_effects=True, vmem_limit_bytes=VMEM_LIMIT),
        name="share",
    )(values)


def live_list(header, live, capacity):
    def check(d, n):
        for j in range(capacity):
            live[n] = d * capacity + j
            n = n + jnp.where(header[d, 0, j] >= 0, 1, 0)
        return n

    return lax.fori_loop(0, header.shape[0], check, jnp.int32(0))


def particle(recv, capacity, s):
    d = s // capacity
    j = s % capacity

    def spread(which):
        return recv[d, pl.ds(which * capacity + j, 8, stride=0), :]

    frac_x = spread(0)
    frac_y = spread(1)
    weight = spread(2)
    cell = spread(3).astype(jnp.int32)
    column = cell & (NG - 1)
    after = (column + 1) & (NG - 1)
    row = cell >> (NG.bit_length() - 1)
    left = (1.0 - frac_x).astype(jnp.bfloat16).astype(jnp.float32)
    right = frac_x.astype(jnp.bfloat16).astype(jnp.float32)
    return frac_y, weight, row, column, after, left, right


def dot3(a_high, a_low, b_high, b_low):
    dot = functools.partial(jnp.dot, preferred_element_type=jnp.float32)
    return dot(a_high, b_high) + (dot(a_high, b_low) + dot(a_low, b_high))


def split(values):
    high = values.astype(jnp.bfloat16)
    return high, (values - high.astype(jnp.float32)).astype(jnp.bfloat16)


def deposit_kernel(capacity, rows, header_h, recv_h, table_high_h, table_low_h, lines_h, spectrum, edges,
                   live, dens, hi, lo, tails, header, recv, table_high, table_low, lines, sems):
    copies = fetch(
        (header_h, recv_h, table_high_h, table_low_h, lines_h),
        (header, recv.at[:, 0 : 4 * capacity], table_high, table_low, lines),
        sems,
    )
    dens[...] = jnp.zeros(dens.shape, jnp.float32)
    tails[...] = jnp.zeros(tails.shape, jnp.float32)
    copies[0].wait()
    n_live = live_list(header, live, capacity)
    copies[1].wait()
    sub8 = lax.broadcasted_iota(jnp.int32, (8, LANES), 0)
    places = [sub8 + 8 * b for b in range(LANES // 8)]

    def one(slot_at):
        alive = slot_at < n_live
        s = live[jnp.where(alive, slot_at, 0)]
        frac_y, weight, row, column, after, left, right = particle(recv, capacity, s)
        weight = jnp.where(alive, weight, 0.0)
        lower = (weight * (1.0 - frac_y)).astype(jnp.bfloat16).astype(jnp.float32)
        upper = (weight * frac_y).astype(jnp.bfloat16).astype(jnp.float32)
        main = jnp.where(row == sub8, lower, jnp.where(row + 1 == sub8, upper, 0.0))
        tail = jnp.where(row == 7, upper, 0.0)

        def row_side(chunk):
            tiles = [jnp.where(chunk == a, main, 0.0) for a in range(CHUNKS)]
            tiles += [jnp.where(chunk == sub8, tail, 0.0), jnp.zeros((8, LANES), jnp.float32)]
            return jnp.concatenate(tiles, axis=0).astype(jnp.bfloat16)

        def column_side(lane, factor):
            return jnp.concatenate([jnp.where(lane == b, factor, 0.0) for b in places], axis=0).astype(jnp.bfloat16)

        lhs = jnp.concatenate([row_side(column >> 7), row_side(after >> 7)], axis=1)
        rhs = jnp.concatenate([column_side(column & 127, left), column_side(after & 127, right)], axis=1)
        values = lax.dot_general(lhs, rhs, (((1,), (1,)), ((), ())), preferred_element_type=jnp.float32)
        return jnp.maximum(header[s // capacity, 0, s % capacity], 0), values

    def group(g, carry):
        results = [one(g * UNROLL + k) for k in range(UNROLL)]
        for band, values in results:
            start = pl.multiple_of(band * 8, 8)
            for a in range(CHUNKS):
                dens[pl.ds(start, 8), a * LANES : (a + 1) * LANES] += values[a * 8 : (a + 1) * 8]
            tails[band] += values[CHUNKS * 8 : CHUNKS * 8 + 8]
        return carry

    lax.fori_loop(0, (n_live + UNROLL - 1) // UNROLL, group, 0)

    def carry_row(t, carry):
        start = pl.multiple_of(t * 8 + 8, 8)
        extra = tails[t]
        for a in range(CHUNKS):
            dens[pl.ds(start, 1), a * LANES : (a + 1) * LANES] += extra[a : a + 1]
        return carry

    lax.fori_loop(0, rows // 8, carry_row, 0)
    high, low = split(dens[...])
    hi[...] = high
    lo[...] = low
    width = 256
    for copy in copies[2:]:
        copy.wait()
    for n in range(NG // width):
        cols = slice(n * width, (n + 1) * width)
        values = dot3(hi[...], lo[...], table_high[:, cols], table_low[:, cols])
        spectrum[:, cols] = values[:rows]
        edges[2:3, cols] = values[rows : rows + 1]
    eight = lines[T_EIGHT * 8 : T_EIGHT * 8 + 8]
    tiles = rows // 8

    def fold(t, carry):
        fwd, bwd = carry
        fwd = eight * fwd + spectrum[pl.ds(pl.multiple_of(t * 8, 8), 8), :]
        bwd = eight * bwd + spectrum[pl.ds(pl.multiple_of((tiles - 1 - t) * 8, 8), 8), :]
        return fwd, bwd

    nothing = jnp.zeros((8, NG), jnp.float32)
    fwd, bwd = lax.fori_loop(0, tiles, fold, (nothing, nothing))
    edges[0:1] = jnp.sum(fwd * lines[T_FEND * 8 : T_FEND * 8 + 8], axis=0, keepdims=True)
    edges[1:2] = jnp.sum(bwd * lines[T_BEND * 8 : T_BEND * 8 + 8], axis=0, keepdims=True)
    edges[3:5] = spectrum[0:2]
    edges[5:6] = spectrum[rows - 1 : rows]
    edges[6:8] = jnp.zeros((2, NG), jnp.float32)


def solve_kernel(capacity, rows, place, header_h, recv_h, spectrum_h, gathered_h, table_high_h, table_low_h, lines_h, potential_h, forces,
                 live, wave, hi, lo, field, rim, potential, spectrum, gathered, header, recv, table_high, table_low, lines, sems):
    copies = fetch(
        (lines_h, gathered_h, spectrum_h, table_high_h, table_low_h, header_h, recv_h),
        (lines, gathered, spectrum, table_high, table_low, header, recv.at[:, 0 : 4 * capacity]),
        sems,
    )
    for copy in copies[:3]:
        copy.wait()
    pens = gathered.shape[0]
    mine = place[0]

    def table(which):
        return lines[which * 8 : which * 8 + 8]

    def row_of(pen, which):
        return gathered[lax.rem(pen + 2 * pens, pens), which : which + 1]

    last_power = table(T_LAST)[0:1]
    before = jnp.zeros((1, NG), jnp.float32)
    beyond = jnp.zeros((1, NG), jnp.float32)
    for j in range(pens):
        lag = lines[T_LAG * 8 + j : T_LAG * 8 + j + 1]
        behind, ahead = mine - 1 - j, mine + 1 + j
        before += lag * (row_of(behind, 0) + last_power * row_of(behind - 1, 2))
        beyond += lag * (row_of(ahead, 1) + row_of(ahead - 1, 2))
    incoming = row_of(mine - 1, 2)
    next_zero = row_of(mine + 1, 3) + row_of(mine, 2)
    next_one = row_of(mine + 1, 4)
    last_before = row_of(mine - 1, 5)
    spectrum_first = spectrum[0:1] + incoming
    first_row = lax.broadcasted_iota(jnp.int32, (8, NG), 0) == 0
    tiles = rows // 8

    def tile_of(t):
        values = spectrum[pl.ds(pl.multiple_of(t * 8, 8), 8), :]
        return values + jnp.where(first_row & (t == 0), incoming, 0.0)

    def backward(i, carry):
        t = tiles - 1 - i
        x = tile_of(t)
        x = x + table(T_B1) * pltpu.roll(x, 7, 0)
        x = x + table(T_B2) * pltpu.roll(x, 6, 0)
        x = x + table(T_B4) * pltpu.roll(x, 4, 0)
        x = x + table(T_BC) * carry
        wave[pl.ds(pl.multiple_of(t * 8 + 8, 8), 8), :] = x
        return x[0:1]

    first_back = lax.fori_loop(0, tiles, backward, beyond)
    norm = table(T_NORM)[0:1]

    def forward(t, carry):
        d = tile_of(t)
        x = d + table(T_F1) * pltpu.roll(d, 1, 0)
        x = x + table(T_F2) * pltpu.roll(x, 2, 0)
        x = x + table(T_F4) * pltpu.roll(x, 4, 0)
        x = x + table(T_FC) * carry
        where = pl.ds(pl.multiple_of(t * 8 + 8, 8), 8)
        wave[where, :] = table(T_NORM) * (x + wave[where, :] - d)
        return x[7:8]

    final = lax.fori_loop(0, tiles, forward, before)
    diagonal = table(T_DIAG)[0:1]
    root = table(T_FC)[0:1]
    scale = 1.0 / NG
    up1 = norm * (before + root * first_back)
    up2 = diagonal * up1 - wave[8:9] - scale * last_before
    down0 = norm * (root * final + beyond)
    down1 = diagonal * down0 - wave[rows + 7 : rows + 8] - scale * next_zero
    down2 = diagonal * down1 - down0 - scale * next_one
    wave[0:6] = jnp.zeros((6, NG), jnp.float32)
    wave[6:7] = up2
    wave[7:8] = up1
    wave[rows + 8 : rows + 9] = down0
    wave[rows + 9 : rows + 10] = down1
    wave[rows + 10 : rows + 11] = down2
    wave[rows + 11 : rows + 16] = jnp.zeros((5, NG), jnp.float32)
    high, low = split(wave[...])
    hi[...] = high
    lo[...] = low
    width = 256
    for copy in copies[3:5]:
        copy.wait()
    for n in range(NG // width):
        cols = slice(n * width, (n + 1) * width)
        wave[:, cols] = dot3(hi[...], lo[...], table_high[:, cols], table_low[:, cols])
    potential[...] = wave[8 : rows + 8]
    out_copy = pltpu.make_async_copy(potential, potential_h, sems.at[7])
    out_copy.start()

    def derive(t, carry):
        base = pl.multiple_of(t * 8, 8)
        tall = jnp.concatenate(
            [
                wave[pl.ds(base, 8), :],
                wave[pl.ds(pl.multiple_of(base + 8, 8), 8), :],
                wave[pl.ds(pl.multiple_of(jnp.minimum(base + 16, rows + 8), 8), 8), :],
            ],
            axis=0,
        )
        middle = tall[8:16]
        along_x = (8.0 * (pltpu.roll(middle, NG - 1, 1) - pltpu.roll(middle, 1, 1))
                   - (pltpu.roll(middle, NG - 2, 1) - pltpu.roll(middle, 2, 1))) / -12.0
        along_y = (8.0 * (tall[9:17] - tall[7:15]) - (tall[10:18] - tall[6:14])) / -12.0

        @pl.when(t < tiles)
        def _():
            field[t, 0:8, :] = along_x
            field[t, 8:16, :] = along_y

        @pl.when(t > 0)
        def _():
            for a in range(CHUNKS):
                lanes = slice(a * LANES, (a + 1) * LANES)
                rim[t - 1, 2 * a : 2 * a + 1, :] = along_x[0:1, lanes]
                rim[t - 1, 2 * a + 1 : 2 * a + 2, :] = along_y[0:1, lanes]

        return carry

    lax.fori_loop(0, tiles + 1, derive, 0)
    for copy in copies[5:]:
        copy.wait()
    n_live = live_list(header, live, capacity)
    forces[...] = jnp.zeros(forces.shape, jnp.float32)
    sub8 = lax.broadcasted_iota(jnp.int32, (8, LANES), 0)

    def pick(values, index):
        return jnp.take_along_axis(values, index, axis=1, mode="promise_in_bounds")

    def one(slot_at):
        s = live[jnp.minimum(slot_at, n_live - 1)]
        band = header[s // capacity, 0, s % capacity]
        frac_y, weight, row, column, after, left, right = particle(recv, capacity, s)
        index = column & 127
        index_after = after & 127
        chunk = column >> 7
        chunk_after = after >> 7
        here = [chunk == a for a in range(1, CHUNKS)]
        there = [chunk_after == a for a in range(1, CHUNKS)]
        row_weight = weight * jnp.where(row == sub8, 1.0 - frac_y, jnp.where(row + 1 == sub8, frac_y, 0.0))
        mixed = []
        for part in range(2):
            for a in range(CHUNKS):
                values = field[band, part * 8 : part * 8 + 8, a * LANES : (a + 1) * LANES]
                g, h = pick(values, index), pick(values, index_after)
                near = g if a == 0 else jnp.where(here[a - 1], g, near)
                far = h if a == 0 else jnp.where(there[a - 1], h, far)
            mixed.append(row_weight * (left * near + right * far))
        edge = weight * jnp.where(row == 7, frac_y, 0.0)
        pair = sub8 >> 1
        rims = jnp.zeros((8, LANES), jnp.float32)
        for half in range(2):
            values = rim[band, half * 8 : half * 8 + 8, :]
            spot = pair + half * 4
            rims += jnp.where(spot == chunk, left * pick(values, index), 0.0)
            rims += jnp.where(spot == chunk_after, right * pick(values, index_after), 0.0)
        rims = edge * rims
        odd = (sub8 & 1) == 1
        out = [
            jnp.sum(mixed[0] + jnp.where(odd, 0.0, rims), axis=0, keepdims=True),
            jnp.sum(mixed[1] + jnp.where(odd, rims, 0.0), axis=0, keepdims=True),
        ]
        return s, out

    def group(g, carry):
        results = [one(g * UNROLL + k) for k in range(UNROLL)]
        for s, values in results:
            d = s // capacity
            j = s % capacity
            forces[d, pl.ds(j, 1), :] = values[0]
            forces[d, pl.ds(capacity + j, 1), :] = values[1]
        return carry

    lax.fori_loop(0, (n_live + UNROLL - 1) // UNROLL, group, 0)
    out_copy.wait()


def unpack_kernel(capacity, target, returned, out):
    def take(i, carry):
        d = target[i] // capacity
        j = target[i] % capacity
        out[i, 0:1, :] = returned[d, pl.ds(j, 1), :]
        out[i, 1:2, :] = returned[d, pl.ds(capacity + j, 1), :]
        return carry

    lax.fori_loop(0, out.shape[0], take, 0, unroll=4)


def shards(block_owner, block_band, block_count, cells, offsets, charges):
    plane_count = lax.axis_size("pln")
    pen_count = lax.axis_size("pen")
    devices = plane_count * pen_count
    local_blocks, block_len = charges.shape
    capacity = max(2, 2 * local_blocks // devices)
    total = devices * capacity
    rows = NG // pen_count
    tall = 4 * capacity
    tall_back = round_up(2 * capacity, 8)
    smem = pl.BlockSpec(memory_space=pltpu.SMEM)
    vmem = pl.BlockSpec(memory_space=pltpu.VMEM)
    far = pl.BlockSpec(memory_space=pltpu.HBM)
    params = pltpu.CompilerParams(vmem_limit_bytes=VMEM_LIMIT)
    packed, header, target = pl.pallas_call(
        functools.partial(pack_kernel, capacity),
        out_shape=(
            jax.ShapeDtypeStruct((devices, tall, LANES), jnp.float32),
            jax.ShapeDtypeStruct((devices, 1, LANES), jnp.int32),
            jax.ShapeDtypeStruct((local_blocks,), jnp.int32),
        ),
        in_specs=[far] * 6,
        out_specs=(vmem, vmem, smem),
        scratch_shapes=[pltpu.SMEM((local_blocks,), jnp.int32)] * 3
        + [
            pltpu.VMEM(cells.shape, jnp.int32),
            pltpu.VMEM(offsets.shape, jnp.float32),
            pltpu.VMEM(charges.shape, jnp.float32),
            pltpu.SMEM((devices,), jnp.int32),
            pltpu.SemaphoreType.DMA((6,)),
        ],
        compiler_params=params,
        name="pack",
    )(block_owner[:, 0], block_band, block_count, cells, offsets, charges)
    received, header = exchange((packed, header), plane_count, pen_count, 0)
    table_high, table_low = (jnp.asarray(t) for t in hartley_tables())
    lines = jnp.asarray(line_tables(pen_count))
    arrived = [
        pltpu.SMEM(header.shape, jnp.int32),
        pltpu.VMEM((devices, tall + 8, LANES), jnp.float32),
    ]
    table_scratch = [
        pltpu.VMEM((NG, NG), jnp.bfloat16),
        pltpu.VMEM((NG, NG), jnp.bfloat16),
        pltpu.VMEM(lines.shape, jnp.float32),
        pltpu.SemaphoreType.DMA((8,)),
    ]
    spectrum, edges = pl.pallas_call(
        functools.partial(deposit_kernel, capacity, rows),
        out_shape=(
            jax.ShapeDtypeStruct((rows, NG), jnp.float32),
            jax.ShapeDtypeStruct((8, NG), jnp.float32),
        ),
        in_specs=[far] * 5,
        out_specs=(vmem, vmem),
        scratch_shapes=[
            pltpu.SMEM((total + 8,), jnp.int32),
            pltpu.VMEM((rows + 8, NG), jnp.float32),
            pltpu.VMEM((rows + 8, NG), jnp.bfloat16),
            pltpu.VMEM((rows + 8, NG), jnp.bfloat16),
            pltpu.VMEM((rows // 8, 8, LANES), jnp.float32),
        ]
        + arrived
        + table_scratch,
        compiler_params=params,
        name="deposit",
    )(header, received, table_high, table_low, lines)
    gathered = share(edges, pen_count, 1)
    place = lax.axis_index("pen").astype(jnp.int32).reshape(1)
    potential, slot_forces = pl.pallas_call(
        functools.partial(solve_kernel, capacity, rows),
        out_shape=(
            jax.ShapeDtypeStruct((rows, NG), jnp.float32),
            jax.ShapeDtypeStruct((devices, tall_back, LANES), jnp.float32),
        ),
        in_specs=[smem] + [far] * 7,
        out_specs=(far, vmem),
        scratch_shapes=[
            pltpu.SMEM((total + 8,), jnp.int32),
            pltpu.VMEM((rows + 16, NG), jnp.float32),
            pltpu.VMEM((rows + 16, NG), jnp.bfloat16),
            pltpu.VMEM((rows + 16, NG), jnp.bfloat16),
            pltpu.VMEM((rows // 8, 16, NG), jnp.float32),
            pltpu.VMEM((rows // 8, 16, LANES), jnp.float32),
            pltpu.VMEM((rows, NG), jnp.float32),
            pltpu.VMEM((rows, NG), jnp.float32),
            pltpu.VMEM(gathered.shape, jnp.float32),
        ]
        + arrived
        + table_scratch,
        compiler_params=params,
        name="solve",
    )(place, header, received, spectrum, gathered, table_high, table_low, lines)
    (returned,) = exchange((slot_forces,), plane_count, pen_count, 2)
    forces = pl.pallas_call(
        functools.partial(unpack_kernel, capacity),
        out_shape=jax.ShapeDtypeStruct((local_blocks, 2, block_len), jnp.float32),
        in_specs=[smem, vmem],
        out_specs=vmem,
        compiler_params=params,
        name="unpack",
    )(target, returned)
    return (potential[None], forces)


def solution(mesh):
    placed = (
        P(("pln", "pen"), None),
        P(("pln", "pen")),
        P(("pln", "pen")),
        P(("pln", "pen"), None),
        P(("pln", "pen"), None, None),
        P(("pln", "pen"), None),
    )
    return jax.shard_map(
        shards,
        mesh=mesh,
        in_specs=placed,
        out_specs=(P("pln", "pen", None), P(("pln", "pen"), None, None)),
        check_vma=False,
    )
```

```python
import functools
import math

import jax
import jax.numpy as jnp
import numpy as np
from jax import lax
from jax.experimental import pallas as pl
from jax.experimental.pallas import tpu as pltpu
from jax.sharding import PartitionSpec as P

NG = 1024
LANES = 128
CHUNKS = NG // LANES
screening = 2e-05
VMEM_LIMIT = 62 * 1024 * 1024
UNROLL = 4


def round_up(value, step):
    return -(-value // step) * step


@functools.lru_cache(None)
def hartley_tables():
    index = np.arange(NG)
    angle = 2.0 * np.pi / NG * (index[:, None] * index[None, :] % NG)
    table = np.cos(angle) + np.sin(angle)
    high = table.astype(jnp.bfloat16)
    low = (table - high.astype(np.float64)).astype(jnp.bfloat16)
    return high, low


@functools.lru_cache(None)
def line_tables(pen_count):
    rows = NG // pen_count
    shift = 4.0 * np.sin(np.pi * np.arange(NG) / NG) ** 2 + screening
    root = 1.0 + shift / 2.0 - np.sqrt(shift + shift * shift / 4.0)
    i = np.arange(8)[:, None]

    def power(exponent):
        return root[None, :] ** (exponent + np.zeros((8, 1)))

    tiles = [
        power(7 - i),
        power(i),
        power(8),
        np.where(i >= 1, power(1), 0.0),
        np.where(i >= 2, power(2), 0.0),
        np.where(i >= 4, power(4), 0.0),
        np.where(i <= 6, power(1), 0.0),
        np.where(i <= 5, power(2), 0.0),
        np.where(i <= 3, power(4), 0.0),
        power(i + 1),
        power(8 - i),
        np.broadcast_to(1.0 / ((1.0 / root - root) * NG), (8, NG)),
        np.broadcast_to(2.0 + shift, (8, NG)),
        power(rows - 1),
    ]
    lags = np.arange(round_up(pen_count, 8))[:, None]
    tiles.append(root[None, :] ** (lags * rows) / (1.0 - root[None, :] ** NG))
    return np.concatenate(tiles, axis=0).astype(np.float32)


T_FEND, T_BEND, T_EIGHT, T_F1, T_F2, T_F4, T_B1, T_B2, T_B4, T_FC, T_BC, T_NORM, T_DIAG, T_LAST, T_LAG = range(15)


def fetch(sources, targets, sems):
    copies = [pltpu.make_async_copy(a, b, sems.at[i]) for i, (a, b) in enumerate(zip(sources, targets))]
    for copy in copies:
        copy.start()
    return copies


def pack_kernel(capacity, owner_h, band_h, count_h, cells_h, offsets_h, charges_h, out, header, target,
                owner, band, count, cells, offsets, charges, used, sems):
    devices = out.shape[0]
    copies = fetch(
        (owner_h, band_h, count_h, cells_h, offsets_h, charges_h),
        (owner, band, count, cells, offsets, charges),
        sems,
    )
    out[...] = jnp.zeros(out.shape, jnp.float32)
    header[...] = jnp.full(header.shape, -1, jnp.int32)

    def clear(i, carry):
        used[i] = 0
        return carry

    lax.fori_loop(0, devices, clear, 0)
    lane = lax.broadcasted_iota(jnp.int32, (1, LANES), 1)
    for copy in copies:
        copy.wait()

    def place(i, carry):
        o = owner[i]
        j = used[o]
        used[o] = j + 1
        target[i] = o * capacity + j
        pair = offsets[i]
        out[o, pl.ds(j, 1), :] = pair[0:1]
        out[o, pl.ds(capacity + j, 1), :] = pair[1:2]
        out[o, pl.ds(2 * capacity + j, 1), :] = jnp.where(lane < count[i], charges[pl.ds(i, 1), :], 0.0)
        out[o, pl.ds(3 * capacity + j, 1), :] = cells[pl.ds(i, 1), :].astype(jnp.float32)
        header[o] = jnp.where(lane == j, band[i], header[o])
        return carry

    lax.fori_loop(0, owner.shape[0], place, 0)


def peer(index, pens):
    return (lax.div(index, pens), lax.rem(index, pens))


def exchange_kernel(planes, pens, arrays, *refs):
    sources, targets = refs[:arrays], refs[arrays : 2 * arrays]
    send_sems, recv_sems, own_sems = refs[2 * arrays :]
    count = planes * pens
    me = lax.axis_index("pln") * pens + lax.axis_index("pen")
    barrier = pltpu.get_barrier_semaphore()

    def greet(k, carry):
        other = peer(lax.rem(me + k, count), pens)
        pl.semaphore_signal(barrier, inc=1, device_id=other, device_id_type=pl.DeviceIdType.MESH)
        return carry

    own = [
        pltpu.make_async_copy(sources[n].at[me], targets[n].at[me], own_sems.at[n]) for n in range(arrays)
    ]
    for copy in own:
        copy.start()
    lax.fori_loop(1, count, greet, 0)
    pl.semaphore_wait(barrier, count - 1)

    def copy_of(n, k, source, target, other):
        return pltpu.make_async_remote_copy(
            src_ref=sources[n].at[source],
            dst_ref=targets[n].at[target],
            send_sem=send_sems.at[n, k],
            recv_sem=recv_sems.at[n, k],
            device_id=peer(other, pens),
            device_id_type=pl.DeviceIdType.MESH,
        )

    def send(k, carry):
        to = lax.rem(me + k, count)
        for n in range(arrays):
            copy_of(n, k, to, me, to).start()
        return carry

    def finish(k, carry):
        to = lax.rem(me + k, count)
        behind = lax.rem(me - k + count, count)
        for n in range(arrays):
            copy_of(n, k, to, me, to).wait_send()
            copy_of(n, k, me, behind, behind).wait_recv()
        return carry

    lax.fori_loop(1, count, send, 0)
    lax.fori_loop(1, count, finish, 0)
    for copy in own:
        copy.wait()


def exchange(values, planes, pens, number):
    place = pl.BlockSpec(memory_space=pl.ANY)
    arrays = len(values)
    return pl.pallas_call(
        functools.partial(exchange_kernel, planes, pens, arrays),
        out_shape=tuple(jax.ShapeDtypeStruct(v.shape, v.dtype) for v in values),
        in_specs=[place] * arrays,
        out_specs=(place,) * arrays,
        scratch_shapes=[
            pltpu.SemaphoreType.DMA((arrays, planes * pens)),
            pltpu.SemaphoreType.DMA((arrays, planes * pens)),
            pltpu.SemaphoreType.DMA((arrays,)),
        ],
        compiler_params=pltpu.CompilerParams(
            collective_id=number, has_side_effects=True, vmem_limit_bytes=VMEM_LIMIT
        ),
        name="exchange",
    )(*values)


def share_kernel(pens, source, target, send_sems, recv_sems, own_sem):
    mine = lax.axis_index("pen")
    plane = lax.axis_index("pln")
    barrier = pltpu.get_barrier_semaphore()
    own = pltpu.make_async_copy(source, target.at[mine], own_sem)
    own.start()
    for k in range(1, pens):
        other = (plane, lax.rem(mine + k, pens))
        pl.semaphore_signal(barrier, inc=1, device_id=other, device_id_type=pl.DeviceIdType.MESH)
    pl.semaphore_wait(barrier, pens - 1)
    sends = []
    for k in range(1, pens):
        copy = pltpu.make_async_remote_copy(
            src_ref=source,
            dst_ref=target.at[mine],
            send_sem=send_sems.at[k],
            recv_sem=recv_sems.at[k],
            device_id=(plane, lax.rem(mine + k, pens)),
            device_id_type=pl.DeviceIdType.MESH,
        )
        copy.start()
        sends.append(copy)
    for k in range(1, pens):
        sends[k - 1].wait_send()
        behind = lax.rem(mine - k + pens, pens)
        pltpu.make_async_remote_copy(
            src_ref=source,
            dst_ref=target.at[behind],
            send_sem=send_sems.at[k],
            recv_sem=recv_sems.at[k],
            device_id=(plane, behind),
            device_id_type=pl.DeviceIdType.MESH,
        ).wait_recv()
    own.wait()


def share(values, pens, number):
    place = pl.BlockSpec(memory_space=pltpu.VMEM)
    return pl.pallas_call(
        functools.partial(share_kernel, pens),
        out_shape=jax.ShapeDtypeStruct((pens,) + values.shape, values.dtype),
        in_specs=[place],
        out_specs=place,
        scratch_shapes=[
            pltpu.SemaphoreType.DMA((pens,)),
            pltpu.SemaphoreType.DMA((pens,)),
            pltpu.SemaphoreType.DMA,
        ],
        compiler_params=pltpu.CompilerParams(collective_id=number, has_side_effects=True, vmem_limit_bytes=VMEM_LIMIT),
        name="share",
    )(values)


def live_list(header, live, capacity):
    def check(d, n):
        for j in range(capacity):
            live[n] = d * capacity + j
            n = n + jnp.where(header[d, 0, j] >= 0, 1, 0)
        return n

    return lax.fori_loop(0, header.shape[0], check, jnp.int32(0))


def particle(recv, capacity, s):
    d = s // capacity
    j = s % capacity

    def spread(which):
        return recv[d, pl.ds(which * capacity + j, 8, stride=0), :]

    return factors(spread(0), spread(1), spread(2), spread(3))


def factors(frac_x, frac_y, weight, cell):
    cell = cell.astype(jnp.int32)
    column = cell & (NG - 1)
    after = (column + 1) & (NG - 1)
    row = cell >> (NG.bit_length() - 1)
    left = (1.0 - frac_x).astype(jnp.bfloat16).astype(jnp.float32)
    right = frac_x.astype(jnp.bfloat16).astype(jnp.float32)
    return frac_y, weight, row, column, after, left, right


def dot3(a_high, a_low, b_high, b_low):
    dot = functools.partial(jnp.dot, preferred_element_type=jnp.float32)
    return dot(a_high, b_high) + (dot(a_high, b_low) + dot(a_low, b_high))


def split(values):
    high = values.astype(jnp.bfloat16)
    return high, (values - high.astype(jnp.float32)).astype(jnp.bfloat16)


def deposit_kernel(capacity, rows, header_h, recv_h, table_high_h, table_low_h, lines_h, spectrum, edges,
                   live, dens, hi, lo, tails, header, recv, table_high, table_low, lines, sems):
    copies = fetch(
        (header_h, recv_h, table_high_h, table_low_h, lines_h),
        (header, recv.at[:, 0 : 4 * capacity], table_high, table_low, lines),
        sems,
    )
    dens[...] = jnp.zeros(dens.shape, jnp.float32)
    tails[...] = jnp.zeros(tails.shape, jnp.float32)
    copies[0].wait()
    n_live = live_list(header, live, capacity)
    copies[1].wait()
    sub8 = lax.broadcasted_iota(jnp.int32, (8, LANES), 0)
    places = [sub8 + 8 * b for b in range(LANES // 8)]

    def one(slot_at):
        alive = slot_at < n_live
        s = live[jnp.where(alive, slot_at, 0)]
        frac_y, weight, row, column, after, left, right = particle(recv, capacity, s)
        weight = jnp.where(alive, weight, 0.0)
        lower = (weight * (1.0 - frac_y)).astype(jnp.bfloat16).astype(jnp.float32)
        upper = (weight * frac_y).astype(jnp.bfloat16).astype(jnp.float32)
        main = jnp.where(row == sub8, lower, jnp.where(row + 1 == sub8, upper, 0.0))
        tail = jnp.where(row == 7, upper, 0.0)

        def row_side(chunk):
            tiles = [jnp.where(chunk == a, main, 0.0) for a in range(CHUNKS)]
            tiles += [jnp.where(chunk == sub8, tail, 0.0), jnp.zeros((8, LANES), jnp.float32)]
            return jnp.concatenate(tiles, axis=0).astype(jnp.bfloat16)

        def column_side(lane, factor):
            return jnp.concatenate([jnp.where(lane == b, factor, 0.0) for b in places], axis=0).astype(jnp.bfloat16)

        lhs = jnp.concatenate([row_side(column >> 7), row_side(after >> 7)], axis=1)
        rhs = jnp.concatenate([column_side(column & 127, left), column_side(after & 127, right)], axis=1)
        values = lax.dot_general(lhs, rhs, (((1,), (1,)), ((), ())), preferred_element_type=jnp.float32)
        return jnp.maximum(header[s // capacity, 0, s % capacity], 0), values

    def group(g, carry):
        results = [one(g * UNROLL + k) for k in range(UNROLL)]
        for band, values in results:
            start = pl.multiple_of(band * 8, 8)
            for a in range(CHUNKS):
                dens[pl.ds(start, 8), a * LANES : (a + 1) * LANES] += values[a * 8 : (a + 1) * 8]
            tails[band] += values[CHUNKS * 8 : CHUNKS * 8 + 8]
        return carry

    lax.fori_loop(0, (n_live + UNROLL - 1) // UNROLL, group, 0)

    def carry_row(t, carry):
        start = pl.multiple_of(t * 8 + 8, 8)
        extra = tails[t]
        for a in range(CHUNKS):
            dens[pl.ds(start, 1), a * LANES : (a + 1) * LANES] += extra[a : a + 1]
        return carry

    lax.fori_loop(0, rows // 8, carry_row, 0)
    high, low = split(dens[...])
    hi[...] = high
    lo[...] = low
    width = 256
    for copy in copies[2:]:
        copy.wait()
    for n in range(NG // width):
        cols = slice(n * width, (n + 1) * width)
        values = dot3(hi[...], lo[...], table_high[:, cols], table_low[:, cols])
        spectrum[:, cols] = values[:rows]
        edges[2:3, cols] = values[rows : rows + 1]
    eight = lines[T_EIGHT * 8 : T_EIGHT * 8 + 8]
    tiles = rows // 8

    def fold(t, carry):
        fwd, bwd = carry
        fwd = eight * fwd + spectrum[pl.ds(pl.multiple_of(t * 8, 8), 8), :]
        bwd = eight * bwd + spectrum[pl.ds(pl.multiple_of((tiles - 1 - t) * 8, 8), 8), :]
        return fwd, bwd

    nothing = jnp.zeros((8, NG), jnp.float32)
    fwd, bwd = lax.fori_loop(0, tiles, fold, (nothing, nothing))
    edges[0:1] = jnp.sum(fwd * lines[T_FEND * 8 : T_FEND * 8 + 8], axis=0, keepdims=True)
    edges[1:2] = jnp.sum(bwd * lines[T_BEND * 8 : T_BEND * 8 + 8], axis=0, keepdims=True)
    edges[3:5] = spectrum[0:2]
    edges[5:6] = spectrum[rows - 1 : rows]
    edges[6:8] = jnp.zeros((2, NG), jnp.float32)


def solve_kernel(rows, place, spectrum_h, gathered_h, table_high_h, table_low_h, lines_h, potential_h, field_h, rim,
                 wave, hi, lo, field, potential, spectrum, gathered, table_high, table_low, lines, sems):
    copies = fetch(
        (lines_h, gathered_h, spectrum_h, table_high_h, table_low_h),
        (lines, gathered, spectrum, table_high, table_low),
        sems,
    )
    for copy in copies[:3]:
        copy.wait()
    pens = gathered.shape[0]
    mine = place[0]

    def table(which):
        return lines[which * 8 : which * 8 + 8]

    def row_of(pen, which):
        return gathered[lax.rem(pen + 2 * pens, pens), which : which + 1]

    last_power = table(T_LAST)[0:1]
    before = jnp.zeros((1, NG), jnp.float32)
    beyond = jnp.zeros((1, NG), jnp.float32)
    for j in range(pens):
        lag = lines[T_LAG * 8 + j : T_LAG * 8 + j + 1]
        behind, ahead = mine - 1 - j, mine + 1 + j
        before += lag * (row_of(behind, 0) + last_power * row_of(behind - 1, 2))
        beyond += lag * (row_of(ahead, 1) + row_of(ahead - 1, 2))
    incoming = row_of(mine - 1, 2)
    next_zero = row_of(mine + 1, 3) + row_of(mine, 2)
    next_one = row_of(mine + 1, 4)
    last_before = row_of(mine - 1, 5)
    spectrum_first = spectrum[0:1] + incoming
    first_row = lax.broadcasted_iota(jnp.int32, (8, NG), 0) == 0
    tiles = rows // 8

    def tile_of(t):
        values = spectrum[pl.ds(pl.multiple_of(t * 8, 8), 8), :]
        return values + jnp.where(first_row & (t == 0), incoming, 0.0)

    def backward(i, carry):
        t = tiles - 1 - i
        x = tile_of(t)
        x = x + table(T_B1) * pltpu.roll(x, 7, 0)
        x = x + table(T_B2) * pltpu.roll(x, 6, 0)
        x = x + table(T_B4) * pltpu.roll(x, 4, 0)
        x = x + table(T_BC) * carry
        wave[pl.ds(pl.multiple_of(t * 8 + 8, 8), 8), :] = x
        return x[0:1]

    first_back = lax.fori_loop(0, tiles, backward, beyond)
    norm = table(T_NORM)[0:1]

    def forward(t, carry):
        d = tile_of(t)
        x = d + table(T_F1) * pltpu.roll(d, 1, 0)
        x = x + table(T_F2) * pltpu.roll(x, 2, 0)
        x = x + table(T_F4) * pltpu.roll(x, 4, 0)
        x = x + table(T_FC) * carry
        where = pl.ds(pl.multiple_of(t * 8 + 8, 8), 8)
        wave[where, :] = table(T_NORM) * (x + wave[where, :] - d)
        return x[7:8]

    final = lax.fori_loop(0, tiles, forward, before)
    diagonal = table(T_DIAG)[0:1]
    root = table(T_FC)[0:1]
    scale = 1.0 / NG
    up1 = norm * (before + root * first_back)
    up2 = diagonal * up1 - wave[8:9] - scale * last_before
    down0 = norm * (root * final + beyond)
    down1 = diagonal * down0 - wave[rows + 7 : rows + 8] - scale * next_zero
    down2 = diagonal * down1 - down0 - scale * next_one
    wave[0:6] = jnp.zeros((6, NG), jnp.float32)
    wave[6:7] = up2
    wave[7:8] = up1
    wave[rows + 8 : rows + 9] = down0
    wave[rows + 9 : rows + 10] = down1
    wave[rows + 10 : rows + 11] = down2
    wave[rows + 11 : rows + 16] = jnp.zeros((5, NG), jnp.float32)
    high, low = split(wave[...])
    hi[...] = high
    lo[...] = low
    width = 256
    for copy in copies[3:5]:
        copy.wait()
    for n in range(NG // width):
        cols = slice(n * width, (n + 1) * width)
        wave[:, cols] = dot3(hi[...], lo[...], table_high[:, cols], table_low[:, cols])
    potential[...] = wave[8 : rows + 8]
    out_copy = pltpu.make_async_copy(potential, potential_h, sems.at[7])
    out_copy.start()

    def derive(t, carry):
        base = pl.multiple_of(t * 8, 8)
        tall = jnp.concatenate(
            [
                wave[pl.ds(base, 8), :],
                wave[pl.ds(pl.multiple_of(base + 8, 8), 8), :],
                wave[pl.ds(pl.multiple_of(jnp.minimum(base + 16, rows + 8), 8), 8), :],
            ],
            axis=0,
        )
        middle = tall[8:16]
        along_x = (8.0 * (pltpu.roll(middle, NG - 1, 1) - pltpu.roll(middle, 1, 1))
                   - (pltpu.roll(middle, NG - 2, 1) - pltpu.roll(middle, 2, 1))) / -12.0
        along_y = (8.0 * (tall[9:17] - tall[7:15]) - (tall[10:18] - tall[6:14])) / -12.0

        @pl.when(t < tiles)
        def _():
            field[t, 0:8, :] = along_x
            field[t, 8:16, :] = along_y
            pltpu.make_async_copy(field.at[t], field_h.at[t], sems.at[6]).start()

        @pl.when(t > 0)
        def _():
            for a in range(CHUNKS):
                lanes = slice(a * LANES, (a + 1) * LANES)
                rim[t - 1, 2 * a : 2 * a + 1, :] = along_x[0:1, lanes]
                rim[t - 1, 2 * a + 1 : 2 * a + 2, :] = along_y[0:1, lanes]

        return carry

    lax.fori_loop(0, tiles + 1, derive, 0)
    pltpu.make_async_copy(field, field_h, sems.at[6]).wait()
    out_copy.wait()


def pull_kernel(planes, pens, capacity, target, header_h, recv_h, field_h, rim_h, out,
                forces, returned, header, recv, field, rim, sems, send_sems, recv_sems):
    count = planes * pens
    me = lax.axis_index("pln") * pens + lax.axis_index("pen")
    barrier = pltpu.get_barrier_semaphore()
    copies = fetch((field_h, header_h, recv_h, rim_h), (field, header, recv, rim), sems)

    def greet(k, carry):
        other = peer(lax.rem(me + k, count), pens)
        pl.semaphore_signal(barrier, inc=1, device_id=other, device_id_type=pl.DeviceIdType.MESH)
        return carry

    lax.fori_loop(1, count, greet, 0)
    for copy in copies:
        copy.wait()
    sub8 = lax.broadcasted_iota(jnp.int32, (8, LANES), 0)
    odd = (sub8 & 1) == 1
    pair = sub8 >> 1

    def pick(values, index):
        return jnp.take_along_axis(values, index, axis=1, mode="promise_in_bounds")

    def one(d, j):
        def spread(which):
            at = which * capacity + j
            return jnp.broadcast_to(recv[d, at : at + 1, :], (8, LANES))

        band = jnp.maximum(header[d, 0, j], 0)
        frac_y, weight, row, column, after, left, right = factors(
            spread(0), spread(1), spread(2), spread(3)
        )
        index = column & 127
        index_after = after & 127
        chunk = column >> 7
        chunk_after = after >> 7
        here = [chunk == a for a in range(1, CHUNKS)]
        there = [chunk_after == a for a in range(1, CHUNKS)]
        row_weight = weight * jnp.where(row == sub8, 1.0 - frac_y, jnp.where(row + 1 == sub8, frac_y, 0.0))
        rows_of = field[band]
        mixed = []
        for part in range(2):
            for a in range(CHUNKS):
                values = rows_of[part * 8 : part * 8 + 8, a * LANES : (a + 1) * LANES]
                g, h = pick(values, index), pick(values, index_after)
                near = g if a == 0 else jnp.where(here[a - 1], g, near)
                far = h if a == 0 else jnp.where(there[a - 1], h, far)
            mixed.append(row_weight * (left * near + right * far))
        edge = weight * jnp.where(row == 7, frac_y, 0.0)
        rims = jnp.zeros((8, LANES), jnp.float32)
        rims_of = rim[band]
        for half in range(2):
            values = rims_of[half * 8 : half * 8 + 8]
            spot = pair + half * 4
            rims += jnp.where(spot == chunk, left * pick(values, index), 0.0)
            rims += jnp.where(spot == chunk_after, right * pick(values, index_after), 0.0)
        rims = edge * rims
        return [
            jnp.sum(mixed[0] + jnp.where(odd, 0.0, rims), axis=0, keepdims=True),
            jnp.sum(mixed[1] + jnp.where(odd, rims, 0.0), axis=0, keepdims=True),
        ]

    def pull(d):
        made = [one(d, j) for j in range(capacity)]
        for c in range(2):
            for j in range(capacity):
                forces[d, c * capacity + j : c * capacity + j + 1, :] = made[j][c]
        if forces.shape[1] > 2 * capacity:
            forces[d, 2 * capacity :, :] = jnp.zeros((forces.shape[1] - 2 * capacity, LANES), jnp.float32)

    def copy_of(k, source, place, other):
        return pltpu.make_async_remote_copy(
            src_ref=forces.at[source],
            dst_ref=returned.at[place],
            send_sem=send_sems.at[k],
            recv_sem=recv_sems.at[k],
            device_id=peer(other, pens),
            device_id_type=pl.DeviceIdType.MESH,
        )

    pull(lax.rem(me + 1, count))
    pl.semaphore_wait(barrier, count - 1)

    def step(k, carry):
        to = lax.rem(me + k, count)
        copy_of(k, to, me, to).start()
        pull(lax.rem(me + k + 1, count))
        return carry

    lax.fori_loop(1, count, step, 0)
    returned[me] = forces[me]

    def finish(k, carry):
        to = lax.rem(me + k, count)
        behind = lax.rem(me - k + count, count)
        copy_of(k, to, me, to).wait_send()
        copy_of(k, me, behind, behind).wait_recv()
        return carry

    lax.fori_loop(1, count, finish, 0)

    def take(i, carry):
        d = target[i] // capacity
        j = target[i] % capacity
        out[i, 0:1, :] = returned[d, pl.ds(j, 1), :]
        out[i, 1:2, :] = returned[d, pl.ds(capacity + j, 1), :]
        return carry

    lax.fori_loop(0, out.shape[0], take, 0)


def shards(block_owner, block_band, block_count, cells, offsets, charges):
    plane_count = lax.axis_size("pln")
    pen_count = lax.axis_size("pen")
    devices = plane_count * pen_count
    local_blocks, block_len = charges.shape
    capacity = max(2, 2 * local_blocks // devices)
    total = devices * capacity
    rows = NG // pen_count
    tall = 4 * capacity
    tall_back = round_up(2 * capacity, 8)
    smem = pl.BlockSpec(memory_space=pltpu.SMEM)
    vmem = pl.BlockSpec(memory_space=pltpu.VMEM)
    far = pl.BlockSpec(memory_space=pltpu.HBM)
    params = pltpu.CompilerParams(vmem_limit_bytes=VMEM_LIMIT)
    packed, header, target = pl.pallas_call(
        functools.partial(pack_kernel, capacity),
        out_shape=(
            jax.ShapeDtypeStruct((devices, tall, LANES), jnp.float32),
            jax.ShapeDtypeStruct((devices, 1, LANES), jnp.int32),
            jax.ShapeDtypeStruct((local_blocks,), jnp.int32),
        ),
        in_specs=[far] * 6,
        out_specs=(vmem, vmem, smem),
        scratch_shapes=[pltpu.SMEM((local_blocks,), jnp.int32)] * 3
        + [
            pltpu.VMEM(cells.shape, jnp.int32),
            pltpu.VMEM(offsets.shape, jnp.float32),
            pltpu.VMEM(charges.shape, jnp.float32),
            pltpu.SMEM((devices,), jnp.int32),
            pltpu.SemaphoreType.DMA((6,)),
        ],
        compiler_params=params,
        name="pack",
    )(block_owner[:, 0], block_band, block_count, cells, offsets, charges)
    received, header = exchange((packed, header), plane_count, pen_count, 0)
    table_high, table_low = (jnp.asarray(t) for t in hartley_tables())
    lines = jnp.asarray(line_tables(pen_count))
    arrived = [
        pltpu.SMEM(header.shape, jnp.int32),
        pltpu.VMEM((devices, tall + 8, LANES), jnp.float32),
    ]
    table_scratch = [
        pltpu.VMEM((NG, NG), jnp.bfloat16),
        pltpu.VMEM((NG, NG), jnp.bfloat16),
        pltpu.VMEM(lines.shape, jnp.float32),
        pltpu.SemaphoreType.DMA((8,)),
    ]
    spectrum, edges = pl.pallas_call(
        functools.partial(deposit_kernel, capacity, rows),
        out_shape=(
            jax.ShapeDtypeStruct((rows, NG), jnp.float32),
            jax.ShapeDtypeStruct((8, NG), jnp.float32),
        ),
        in_specs=[far] * 5,
        out_specs=(vmem, vmem),
        scratch_shapes=[
            pltpu.SMEM((total + 8,), jnp.int32),
            pltpu.VMEM((rows + 8, NG), jnp.float32),
            pltpu.VMEM((rows + 8, NG), jnp.bfloat16),
            pltpu.VMEM((rows + 8, NG), jnp.bfloat16),
            pltpu.VMEM((rows // 8, 8, LANES), jnp.float32),
        ]
        + arrived
        + table_scratch,
        compiler_params=params,
        name="deposit",
    )(header, received, table_high, table_low, lines)
    gathered = share(edges, pen_count, 1)
    place = lax.axis_index("pen").astype(jnp.int32).reshape(1)
    potential, field, rim = pl.pallas_call(
        functools.partial(solve_kernel, rows),
        out_shape=(
            jax.ShapeDtypeStruct((rows, NG), jnp.float32),
            jax.ShapeDtypeStruct((rows // 8, 16, NG), jnp.float32),
            jax.ShapeDtypeStruct((rows // 8, 16, LANES), jnp.float32),
        ),
        in_specs=[smem] + [far] * 5,
        out_specs=(far, far, vmem),
        scratch_shapes=[
            pltpu.VMEM((rows + 16, NG), jnp.float32),
            pltpu.VMEM((rows + 16, NG), jnp.bfloat16),
            pltpu.VMEM((rows + 16, NG), jnp.bfloat16),
            pltpu.VMEM((rows // 8, 16, NG), jnp.float32),
            pltpu.VMEM((rows, NG), jnp.float32),
            pltpu.VMEM((rows, NG), jnp.float32),
            pltpu.VMEM(gathered.shape, jnp.float32),
        ]
        + table_scratch,
        compiler_params=params,
        name="solve",
    )(place, spectrum, gathered, table_high, table_low, lines)
    forces = pl.pallas_call(
        functools.partial(pull_kernel, plane_count, pen_count, capacity),
        out_shape=jax.ShapeDtypeStruct((local_blocks, 2, block_len), jnp.float32),
        in_specs=[smem] + [far] * 4,
        out_specs=vmem,
        scratch_shapes=[
            pltpu.VMEM((devices, tall_back, LANES), jnp.float32),
            pltpu.VMEM((devices, tall_back, LANES), jnp.float32),
            pltpu.SMEM(header.shape, jnp.int32),
            pltpu.VMEM(received.shape, jnp.float32),
            pltpu.VMEM(field.shape, jnp.float32),
            pltpu.VMEM(rim.shape, jnp.float32),
            pltpu.SemaphoreType.DMA((4,)),
            pltpu.SemaphoreType.DMA((devices,)),
            pltpu.SemaphoreType.DMA((devices,)),
        ],
        compiler_params=pltpu.CompilerParams(
            collective_id=2, has_side_effects=True, vmem_limit_bytes=VMEM_LIMIT
        ),
        name="pull",
    )(target, header, received, field, rim)
    return (potential[None], forces)


def solution(mesh):
    placed = (
        P(("pln", "pen"), None),
        P(("pln", "pen")),
        P(("pln", "pen")),
        P(("pln", "pen"), None),
        P(("pln", "pen"), None, None),
        P(("pln", "pen"), None),
    )
    return jax.shard_map(
        shards,
        mesh=mesh,
        in_specs=placed,
        out_specs=(P("pln", "pen", None), P(("pln", "pen"), None, None)),
        check_vma=False,
    )
```

```python
import functools
import math

import jax
import jax.numpy as jnp
import numpy as np
from jax import lax
from jax.experimental import pallas as pl
from jax.experimental.pallas import tpu as pltpu
from jax.sharding import PartitionSpec as P

NG = 1024
LANES = 128
CHUNKS = NG // LANES
screening = 2e-05
VMEM_LIMIT = 62 * 1024 * 1024
UNROLL = 4


def round_up(value, step):
    return -(-value // step) * step


@functools.lru_cache(None)
def hartley_tables():
    index = np.arange(NG)
    angle = 2.0 * np.pi / NG * (index[:, None] * index[None, :] % NG)
    table = np.cos(angle) + np.sin(angle)
    high = table.astype(jnp.bfloat16)
    low = (table - high.astype(np.float64)).astype(jnp.bfloat16)
    return high, low


@functools.lru_cache(None)
def line_tables(pen_count):
    rows = NG // pen_count
    shift = 4.0 * np.sin(np.pi * np.arange(NG) / NG) ** 2 + screening
    root = 1.0 + shift / 2.0 - np.sqrt(shift + shift * shift / 4.0)
    i = np.arange(8)[:, None]

    def power(exponent):
        return root[None, :] ** (exponent + np.zeros((8, 1)))

    tiles = [
        power(7 - i),
        power(i),
        power(8),
        np.where(i >= 1, power(1), 0.0),
        np.where(i >= 2, power(2), 0.0),
        np.where(i >= 4, power(4), 0.0),
        np.where(i <= 6, power(1), 0.0),
        np.where(i <= 5, power(2), 0.0),
        np.where(i <= 3, power(4), 0.0),
        power(i + 1),
        power(8 - i),
        np.broadcast_to(1.0 / ((1.0 / root - root) * NG), (8, NG)),
        np.broadcast_to(2.0 + shift, (8, NG)),
        power(rows - 1),
    ]
    lags = np.arange(round_up(pen_count, 8))[:, None]
    tiles.append(root[None, :] ** (lags * rows) / (1.0 - root[None, :] ** NG))
    return np.concatenate(tiles, axis=0).astype(np.float32)


T_FEND, T_BEND, T_EIGHT, T_F1, T_F2, T_F4, T_B1, T_B2, T_B4, T_FC, T_BC, T_NORM, T_DIAG, T_LAST, T_LAG = range(15)


def fetch(sources, targets, sems):
    copies = [pltpu.make_async_copy(a, b, sems.at[i]) for i, (a, b) in enumerate(zip(sources, targets))]
    for copy in copies:
        copy.start()
    return copies


def pack_kernel(capacity, owner_h, band_h, count_h, cells_h, offsets_h, charges_h, out, header, target,
                owner, band, count, cells, offsets, charges, used, sems):
    devices = out.shape[0]
    copies = fetch(
        (owner_h, band_h, count_h, cells_h, offsets_h, charges_h),
        (owner, band, count, cells, offsets, charges),
        sems,
    )
    out[...] = jnp.zeros(out.shape, jnp.float32)
    header[...] = jnp.full(header.shape, -1, jnp.int32)

    def clear(i, carry):
        used[i] = 0
        return carry

    lax.fori_loop(0, devices, clear, 0)
    lane = lax.broadcasted_iota(jnp.int32, (1, LANES), 1)
    for copy in copies:
        copy.wait()

    def place(i, carry):
        o = owner[i]
        j = used[o]
        used[o] = j + 1
        target[i] = o * capacity + j
        pair = offsets[i]
        out[o, pl.ds(j, 1), :] = pair[0:1]
        out[o, pl.ds(capacity + j, 1), :] = pair[1:2]
        out[o, pl.ds(2 * capacity + j, 1), :] = jnp.where(lane < count[i], charges[pl.ds(i, 1), :], 0.0)
        out[o, pl.ds(3 * capacity + j, 1), :] = cells[pl.ds(i, 1), :].astype(jnp.float32)
        header[o] = jnp.where(lane == j, band[i], header[o])
        return carry

    lax.fori_loop(0, owner.shape[0], place, 0)


def peer(index, pens):
    return (lax.div(index, pens), lax.rem(index, pens))


def exchange_kernel(planes, pens, arrays, *refs):
    sources, targets = refs[:arrays], refs[arrays : 2 * arrays]
    send_sems, recv_sems, own_sems = refs[2 * arrays :]
    count = planes * pens
    me = lax.axis_index("pln") * pens + lax.axis_index("pen")
    barrier = pltpu.get_barrier_semaphore()

    def greet(k, carry):
        other = peer(lax.rem(me + k, count), pens)
        pl.semaphore_signal(barrier, inc=1, device_id=other, device_id_type=pl.DeviceIdType.MESH)
        return carry

    own = [
        pltpu.make_async_copy(sources[n].at[me], targets[n].at[me], own_sems.at[n]) for n in range(arrays)
    ]
    for copy in own:
        copy.start()
    lax.fori_loop(1, count, greet, 0)
    pl.semaphore_wait(barrier, count - 1)

    def copy_of(n, k, source, target, other):
        return pltpu.make_async_remote_copy(
            src_ref=sources[n].at[source],
            dst_ref=targets[n].at[target],
            send_sem=send_sems.at[n, k],
            recv_sem=recv_sems.at[n, k],
            device_id=peer(other, pens),
            device_id_type=pl.DeviceIdType.MESH,
        )

    def send(k, carry):
        to = lax.rem(me + k, count)
        for n in range(arrays):
            copy_of(n, k, to, me, to).start()
        return carry

    def finish(k, carry):
        to = lax.rem(me + k, count)
        behind = lax.rem(me - k + count, count)
        for n in range(arrays):
            copy_of(n, k, to, me, to).wait_send()
            copy_of(n, k, me, behind, behind).wait_recv()
        return carry

    lax.fori_loop(1, count, send, 0)
    lax.fori_loop(1, count, finish, 0)
    for copy in own:
        copy.wait()


def exchange(values, planes, pens, number):
    place = pl.BlockSpec(memory_space=pl.ANY)
    arrays = len(values)
    return pl.pallas_call(
        functools.partial(exchange_kernel, planes, pens, arrays),
        out_shape=tuple(jax.ShapeDtypeStruct(v.shape, v.dtype) for v in values),
        in_specs=[place] * arrays,
        out_specs=(place,) * arrays,
        scratch_shapes=[
            pltpu.SemaphoreType.DMA((arrays, planes * pens)),
            pltpu.SemaphoreType.DMA((arrays, planes * pens)),
            pltpu.SemaphoreType.DMA((arrays,)),
        ],
        compiler_params=pltpu.CompilerParams(
            collective_id=number, has_side_effects=True, vmem_limit_bytes=VMEM_LIMIT
        ),
        name="exchange",
    )(*values)


def live_list(header, live, capacity):
    def check(d, n):
        for j in range(capacity):
            live[n] = d * capacity + j
            n = n + jnp.where(header[d, 0, j] >= 0, 1, 0)
        return n

    return lax.fori_loop(0, header.shape[0], check, jnp.int32(0))


def particle(recv, capacity, s):
    d = s // capacity
    j = s % capacity

    def spread(which):
        return recv[d, pl.ds(which * capacity + j, 8, stride=0), :]

    return factors(spread(0), spread(1), spread(2), spread(3))


def factors(frac_x, frac_y, weight, cell):
    cell = cell.astype(jnp.int32)
    column = cell & (NG - 1)
    after = (column + 1) & (NG - 1)
    row = cell >> (NG.bit_length() - 1)
    left = (1.0 - frac_x).astype(jnp.bfloat16).astype(jnp.float32)
    right = frac_x.astype(jnp.bfloat16).astype(jnp.float32)
    return frac_y, weight, row, column, after, left, right


def dot3(a_high, a_low, b_high, b_low):
    dot = functools.partial(jnp.dot, preferred_element_type=jnp.float32)
    return dot(a_high, b_high) + (dot(a_high, b_low) + dot(a_low, b_high))


def split(values):
    high = values.astype(jnp.bfloat16)
    return high, (values - high.astype(jnp.float32)).astype(jnp.bfloat16)


def deposit_kernel(capacity, rows, header_h, recv_h, table_high_h, table_low_h, lines_h, spectrum, edges,
                   live, dens, hi, lo, tails, header, recv, table_high, table_low, lines, sems):
    copies = fetch(
        (header_h, recv_h, table_high_h, table_low_h, lines_h),
        (header, recv.at[:, 0 : 4 * capacity], table_high, table_low, lines),
        sems,
    )
    dens[...] = jnp.zeros(dens.shape, jnp.float32)
    tails[...] = jnp.zeros(tails.shape, jnp.float32)
    copies[0].wait()
    n_live = live_list(header, live, capacity)
    copies[1].wait()
    sub8 = lax.broadcasted_iota(jnp.int32, (8, LANES), 0)
    places = [sub8 + 8 * b for b in range(LANES // 8)]

    def one(slot_at):
        alive = slot_at < n_live
        s = live[jnp.where(alive, slot_at, 0)]
        frac_y, weight, row, column, after, left, right = particle(recv, capacity, s)
        weight = jnp.where(alive, weight, 0.0)
        lower = (weight * (1.0 - frac_y)).astype(jnp.bfloat16).astype(jnp.float32)
        upper = (weight * frac_y).astype(jnp.bfloat16).astype(jnp.float32)
        main = jnp.where(row == sub8, lower, jnp.where(row + 1 == sub8, upper, 0.0))
        tail = jnp.where(row == 7, upper, 0.0)

        def row_side(chunk):
            tiles = [jnp.where(chunk == a, main, 0.0) for a in range(CHUNKS)]
            tiles += [jnp.where(chunk == sub8, tail, 0.0), jnp.zeros((8, LANES), jnp.float32)]
            return jnp.concatenate(tiles, axis=0).astype(jnp.bfloat16)

        def column_side(lane, factor):
            return jnp.concatenate([jnp.where(lane == b, factor, 0.0) for b in places], axis=0).astype(jnp.bfloat16)

        lhs = jnp.concatenate([row_side(column >> 7), row_side(after >> 7)], axis=1)
        rhs = jnp.concatenate([column_side(column & 127, left), column_side(after & 127, right)], axis=1)
        values = lax.dot_general(lhs, rhs, (((1,), (1,)), ((), ())), preferred_element_type=jnp.float32)
        return jnp.maximum(header[s // capacity, 0, s % capacity], 0), values

    def group(g, carry):
        results = [one(g * UNROLL + k) for k in range(UNROLL)]
        for band, values in results:
            start = pl.multiple_of(band * 8, 8)
            for a in range(CHUNKS):
                dens[pl.ds(start, 8), a * LANES : (a + 1) * LANES] += values[a * 8 : (a + 1) * 8]
            tails[band] += values[CHUNKS * 8 : CHUNKS * 8 + 8]
        return carry

    lax.fori_loop(0, (n_live + UNROLL - 1) // UNROLL, group, 0)

    def carry_row(t, carry):
        start = pl.multiple_of(t * 8 + 8, 8)
        extra = tails[t]
        for a in range(CHUNKS):
            dens[pl.ds(start, 1), a * LANES : (a + 1) * LANES] += extra[a : a + 1]
        return carry

    lax.fori_loop(0, rows // 8, carry_row, 0)
    high, low = split(dens[...])
    hi[...] = high
    lo[...] = low
    width = 256
    for copy in copies[2:]:
        copy.wait()
    for n in range(NG // width):
        cols = slice(n * width, (n + 1) * width)
        values = dot3(hi[...], lo[...], table_high[:, cols], table_low[:, cols])
        spectrum[:, cols] = values[:rows]
        edges[2:3, cols] = values[rows : rows + 1]
    eight = lines[T_EIGHT * 8 : T_EIGHT * 8 + 8]
    tiles = rows // 8

    def fold(t, carry):
        fwd, bwd = carry
        fwd = eight * fwd + spectrum[pl.ds(pl.multiple_of(t * 8, 8), 8), :]
        bwd = eight * bwd + spectrum[pl.ds(pl.multiple_of((tiles - 1 - t) * 8, 8), 8), :]
        return fwd, bwd

    nothing = jnp.zeros((8, NG), jnp.float32)
    fwd, bwd = lax.fori_loop(0, tiles, fold, (nothing, nothing))
    edges[0:1] = jnp.sum(fwd * lines[T_FEND * 8 : T_FEND * 8 + 8], axis=0, keepdims=True)
    edges[1:2] = jnp.sum(bwd * lines[T_BEND * 8 : T_BEND * 8 + 8], axis=0, keepdims=True)
    edges[3:5] = spectrum[0:2]
    edges[5:6] = spectrum[rows - 1 : rows]
    edges[6:8] = jnp.zeros((2, NG), jnp.float32)


def solve(rows, mine, copies, potential_h, out_sem, rim, wave, hi, lo, field, potential, spectrum, gathered,
          table_high, table_low, lines):
    pens = gathered.shape[0]
    def table(which):
        return lines[which * 8 : which * 8 + 8]

    def row_of(pen, which):
        return gathered[lax.rem(pen + 2 * pens, pens), which : which + 1]

    last_power = table(T_LAST)[0:1]
    before = jnp.zeros((1, NG), jnp.float32)
    beyond = jnp.zeros((1, NG), jnp.float32)
    for j in range(pens):
        lag = lines[T_LAG * 8 + j : T_LAG * 8 + j + 1]
        behind, ahead = mine - 1 - j, mine + 1 + j
        before += lag * (row_of(behind, 0) + last_power * row_of(behind - 1, 2))
        beyond += lag * (row_of(ahead, 1) + row_of(ahead - 1, 2))
    incoming = row_of(mine - 1, 2)
    next_zero = row_of(mine + 1, 3) + row_of(mine, 2)
    next_one = row_of(mine + 1, 4)
    last_before = row_of(mine - 1, 5)
    spectrum_first = spectrum[0:1] + incoming
    first_row = lax.broadcasted_iota(jnp.int32, (8, NG), 0) == 0
    tiles = rows // 8

    def tile_of(t):
        values = spectrum[pl.ds(pl.multiple_of(t * 8, 8), 8), :]
        return values + jnp.where(first_row & (t == 0), incoming, 0.0)

    def backward(i, carry):
        t = tiles - 1 - i
        x = tile_of(t)
        x = x + table(T_B1) * pltpu.roll(x, 7, 0)
        x = x + table(T_B2) * pltpu.roll(x, 6, 0)
        x = x + table(T_B4) * pltpu.roll(x, 4, 0)
        x = x + table(T_BC) * carry
        wave[pl.ds(pl.multiple_of(t * 8 + 8, 8), 8), :] = x
        return x[0:1]

    first_back = lax.fori_loop(0, tiles, backward, beyond)
    norm = table(T_NORM)[0:1]

    def forward(t, carry):
        d = tile_of(t)
        x = d + table(T_F1) * pltpu.roll(d, 1, 0)
        x = x + table(T_F2) * pltpu.roll(x, 2, 0)
        x = x + table(T_F4) * pltpu.roll(x, 4, 0)
        x = x + table(T_FC) * carry
        where = pl.ds(pl.multiple_of(t * 8 + 8, 8), 8)
        wave[where, :] = table(T_NORM) * (x + wave[where, :] - d)
        return x[7:8]

    final = lax.fori_loop(0, tiles, forward, before)
    diagonal = table(T_DIAG)[0:1]
    root = table(T_FC)[0:1]
    scale = 1.0 / NG
    up1 = norm * (before + root * first_back)
    up2 = diagonal * up1 - wave[8:9] - scale * last_before
    down0 = norm * (root * final + beyond)
    down1 = diagonal * down0 - wave[rows + 7 : rows + 8] - scale * next_zero
    down2 = diagonal * down1 - down0 - scale * next_one
    wave[0:6] = jnp.zeros((6, NG), jnp.float32)
    wave[6:7] = up2
    wave[7:8] = up1
    wave[rows + 8 : rows + 9] = down0
    wave[rows + 9 : rows + 10] = down1
    wave[rows + 10 : rows + 11] = down2
    wave[rows + 11 : rows + 16] = jnp.zeros((5, NG), jnp.float32)
    high, low = split(wave[...])
    hi[...] = high
    lo[...] = low
    width = 256
    for copy in copies:
        copy.wait()
    for n in range(NG // width):
        cols = slice(n * width, (n + 1) * width)
        wave[:, cols] = dot3(hi[...], lo[...], table_high[:, cols], table_low[:, cols])
    potential[...] = wave[8 : rows + 8]
    out_copy = pltpu.make_async_copy(potential, potential_h, out_sem)
    out_copy.start()

    def derive(t, carry):
        base = pl.multiple_of(t * 8, 8)
        tall = jnp.concatenate(
            [
                wave[pl.ds(base, 8), :],
                wave[pl.ds(pl.multiple_of(base + 8, 8), 8), :],
                wave[pl.ds(pl.multiple_of(jnp.minimum(base + 16, rows + 8), 8), 8), :],
            ],
            axis=0,
        )
        middle = tall[8:16]
        along_x = (8.0 * (pltpu.roll(middle, NG - 1, 1) - pltpu.roll(middle, 1, 1))
                   - (pltpu.roll(middle, NG - 2, 1) - pltpu.roll(middle, 2, 1))) / -12.0
        along_y = (8.0 * (tall[9:17] - tall[7:15]) - (tall[10:18] - tall[6:14])) / -12.0

        @pl.when(t < tiles)
        def _():
            field[t, 0:8, :] = along_x
            field[t, 8:16, :] = along_y

        @pl.when(t > 0)
        def _():
            for a in range(CHUNKS):
                lanes = slice(a * LANES, (a + 1) * LANES)
                rim[t - 1, 2 * a : 2 * a + 1, :] = along_x[0:1, lanes]
                rim[t - 1, 2 * a + 1 : 2 * a + 2, :] = along_y[0:1, lanes]

        return carry

    lax.fori_loop(0, tiles + 1, derive, 0)
    return out_copy


def pull_kernel(planes, pens, capacity, rows, target, header_h, recv_h, spectrum_h, edges_h, table_high_h, table_low_h,
                lines_h, potential_h, out, forces, returned, header, recv, field, rim, wave, hi, lo, potential,
                spectrum, edges, gathered, table_high, table_low, lines, sems, send_sems, recv_sems,
                edge_send_sems, edge_recv_sems):
    count = planes * pens
    me = lax.axis_index("pln") * pens + lax.axis_index("pen")
    barrier = pltpu.get_barrier_semaphore()
    copies = fetch(
        (edges_h, lines_h, spectrum_h, table_high_h, table_low_h, header_h, recv_h),
        (edges, lines, spectrum, table_high, table_low, header, recv),
        sems,
    )
    plane = lax.axis_index("pln")
    mine = lax.axis_index("pen")

    def greet(k, carry):
        other = peer(lax.rem(me + k, count), pens)
        pl.semaphore_signal(barrier, inc=1, device_id=other, device_id_type=pl.DeviceIdType.MESH)
        return carry

    lax.fori_loop(1, count, greet, 0)
    for copy in copies[:3]:
        copy.wait()
    gathered[mine] = edges[...]
    pl.semaphore_wait(barrier, count - 1)

    def edge_copy(k, place, other):
        return pltpu.make_async_remote_copy(
            src_ref=edges,
            dst_ref=gathered.at[place],
            send_sem=edge_send_sems.at[k],
            recv_sem=edge_recv_sems.at[k],
            device_id=(plane, other),
            device_id_type=pl.DeviceIdType.MESH,
        )

    for k in range(1, pens):
        edge_copy(k, mine, lax.rem(mine + k, pens)).start()
    for k in range(1, pens):
        behind = lax.rem(mine - k + pens, pens)
        edge_copy(k, mine, lax.rem(mine + k, pens)).wait_send()
        edge_copy(k, behind, behind).wait_recv()
    out_copy = solve(rows, mine, copies[3:5], potential_h, sems.at[7], rim, wave, hi, lo, field, potential, spectrum,
                     gathered, table_high, table_low, lines)
    for copy in copies[5:]:
        copy.wait()
    sub8 = lax.broadcasted_iota(jnp.int32, (8, LANES), 0)
    odd = (sub8 & 1) == 1
    pair = sub8 >> 1

    def pick(values, index):
        return jnp.take_along_axis(values, index, axis=1, mode="promise_in_bounds")

    def one(d, j):
        def spread(which):
            at = which * capacity + j
            return jnp.broadcast_to(recv[d, at : at + 1, :], (8, LANES))

        band = jnp.maximum(header[d, 0, j], 0)
        frac_y, weight, row, column, after, left, right = factors(
            spread(0), spread(1), spread(2), spread(3)
        )
        index = column & 127
        index_after = after & 127
        chunk = column >> 7
        chunk_after = after >> 7
        here = [chunk == a for a in range(1, CHUNKS)]
        there = [chunk_after == a for a in range(1, CHUNKS)]
        row_weight = weight * jnp.where(row == sub8, 1.0 - frac_y, jnp.where(row + 1 == sub8, frac_y, 0.0))
        rows_of = field[band]
        mixed = []
        for part in range(2):
            for a in range(CHUNKS):
                values = rows_of[part * 8 : part * 8 + 8, a * LANES : (a + 1) * LANES]
                g, h = pick(values, index), pick(values, index_after)
                near = g if a == 0 else jnp.where(here[a - 1], g, near)
                far = h if a == 0 else jnp.where(there[a - 1], h, far)
            mixed.append(row_weight * (left * near + right * far))
        edge = weight * jnp.where(row == 7, frac_y, 0.0)
        rims = jnp.zeros((8, LANES), jnp.float32)
        rims_of = rim[band]
        for half in range(2):
            values = rims_of[half * 8 : half * 8 + 8]
            spot = pair + half * 4
            rims += jnp.where(spot == chunk, left * pick(values, index), 0.0)
            rims += jnp.where(spot == chunk_after, right * pick(values, index_after), 0.0)
        rims = edge * rims
        return [
            jnp.sum(mixed[0] + jnp.where(odd, 0.0, rims), axis=0, keepdims=True),
            jnp.sum(mixed[1] + jnp.where(odd, rims, 0.0), axis=0, keepdims=True),
        ]

    def pull(d):
        made = [one(d, j) for j in range(capacity)]
        for c in range(2):
            for j in range(capacity):
                forces[d, c * capacity + j : c * capacity + j + 1, :] = made[j][c]
        if forces.shape[1] > 2 * capacity:
            forces[d, 2 * capacity :, :] = jnp.zeros((forces.shape[1] - 2 * capacity, LANES), jnp.float32)

    def copy_of(k, source, place, other):
        return pltpu.make_async_remote_copy(
            src_ref=forces.at[source],
            dst_ref=returned.at[place],
            send_sem=send_sems.at[k],
            recv_sem=recv_sems.at[k],
            device_id=peer(other, pens),
            device_id_type=pl.DeviceIdType.MESH,
        )

    pull(lax.rem(me + 1, count))

    def step(k, carry):
        to = lax.rem(me + k, count)
        copy_of(k, to, me, to).start()
        pull(lax.rem(me + k + 1, count))
        return carry

    lax.fori_loop(1, count, step, 0)
    returned[me] = forces[me]

    def finish(k, carry):
        to = lax.rem(me + k, count)
        behind = lax.rem(me - k + count, count)
        copy_of(k, to, me, to).wait_send()
        copy_of(k, me, behind, behind).wait_recv()
        return carry

    lax.fori_loop(1, count, finish, 0)

    def take(i, carry):
        d = target[i] // capacity
        j = target[i] % capacity
        out[i, 0:1, :] = returned[d, pl.ds(j, 1), :]
        out[i, 1:2, :] = returned[d, pl.ds(capacity + j, 1), :]
        return carry

    lax.fori_loop(0, out.shape[0], take, 0)
    out_copy.wait()


def shards(block_owner, block_band, block_count, cells, offsets, charges):
    plane_count = lax.axis_size("pln")
    pen_count = lax.axis_size("pen")
    devices = plane_count * pen_count
    local_blocks, block_len = charges.shape
    capacity = max(2, 2 * local_blocks // devices)
    total = devices * capacity
    rows = NG // pen_count
    tall = 4 * capacity
    tall_back = round_up(2 * capacity, 8)
    smem = pl.BlockSpec(memory_space=pltpu.SMEM)
    vmem = pl.BlockSpec(memory_space=pltpu.VMEM)
    far = pl.BlockSpec(memory_space=pltpu.HBM)
    params = pltpu.CompilerParams(vmem_limit_bytes=VMEM_LIMIT)
    packed, header, target = pl.pallas_call(
        functools.partial(pack_kernel, capacity),
        out_shape=(
            jax.ShapeDtypeStruct((devices, tall, LANES), jnp.float32),
            jax.ShapeDtypeStruct((devices, 1, LANES), jnp.int32),
            jax.ShapeDtypeStruct((local_blocks,), jnp.int32),
        ),
        in_specs=[far] * 6,
        out_specs=(vmem, vmem, smem),
        scratch_shapes=[pltpu.SMEM((local_blocks,), jnp.int32)] * 3
        + [
            pltpu.VMEM(cells.shape, jnp.int32),
            pltpu.VMEM(offsets.shape, jnp.float32),
            pltpu.VMEM(charges.shape, jnp.float32),
            pltpu.SMEM((devices,), jnp.int32),
            pltpu.SemaphoreType.DMA((6,)),
        ],
        compiler_params=params,
        name="pack",
    )(block_owner[:, 0], block_band, block_count, cells, offsets, charges)
    received, header = exchange((packed, header), plane_count, pen_count, 0)
    table_high, table_low = (jnp.asarray(t) for t in hartley_tables())
    lines = jnp.asarray(line_tables(pen_count))
    arrived = [
        pltpu.SMEM(header.shape, jnp.int32),
        pltpu.VMEM((devices, tall + 8, LANES), jnp.float32),
    ]
    table_scratch = [
        pltpu.VMEM((NG, NG), jnp.bfloat16),
        pltpu.VMEM((NG, NG), jnp.bfloat16),
        pltpu.VMEM(lines.shape, jnp.float32),
        pltpu.SemaphoreType.DMA((8,)),
    ]
    spectrum, edges = pl.pallas_call(
        functools.partial(deposit_kernel, capacity, rows),
        out_shape=(
            jax.ShapeDtypeStruct((rows, NG), jnp.float32),
            jax.ShapeDtypeStruct((8, NG), jnp.float32),
        ),
        in_specs=[far] * 5,
        out_specs=(vmem, vmem),
        scratch_shapes=[
            pltpu.SMEM((total + 8,), jnp.int32),
            pltpu.VMEM((rows + 8, NG), jnp.float32),
            pltpu.VMEM((rows + 8, NG), jnp.bfloat16),
            pltpu.VMEM((rows + 8, NG), jnp.bfloat16),
            pltpu.VMEM((rows // 8, 8, LANES), jnp.float32),
        ]
        + arrived
        + table_scratch,
        compiler_params=params,
        name="deposit",
    )(header, received, table_high, table_low, lines)
    potential, forces = pl.pallas_call(
        functools.partial(pull_kernel, plane_count, pen_count, capacity, rows),
        out_shape=(
            jax.ShapeDtypeStruct((rows, NG), jnp.float32),
            jax.ShapeDtypeStruct((local_blocks, 2, block_len), jnp.float32),
        ),
        in_specs=[smem] + [far] * 7,
        out_specs=(far, vmem),
        scratch_shapes=[
            pltpu.VMEM((devices, tall_back, LANES), jnp.float32),
            pltpu.VMEM((devices, tall_back, LANES), jnp.float32),
            pltpu.SMEM(header.shape, jnp.int32),
            pltpu.VMEM(received.shape, jnp.float32),
            pltpu.VMEM((rows // 8, 16, NG), jnp.float32),
            pltpu.VMEM((rows // 8, 16, LANES), jnp.float32),
            pltpu.VMEM((rows + 16, NG), jnp.float32),
            pltpu.VMEM((rows + 16, NG), jnp.bfloat16),
            pltpu.VMEM((rows + 16, NG), jnp.bfloat16),
            pltpu.VMEM((rows, NG), jnp.float32),
            pltpu.VMEM((rows, NG), jnp.float32),
            pltpu.VMEM((8, NG), jnp.float32),
            pltpu.VMEM((pen_count, 8, NG), jnp.float32),
        ]
        + table_scratch
        + [
            pltpu.SemaphoreType.DMA((devices,)),
            pltpu.SemaphoreType.DMA((devices,)),
            pltpu.SemaphoreType.DMA((pen_count,)),
            pltpu.SemaphoreType.DMA((pen_count,)),
        ],
        compiler_params=pltpu.CompilerParams(
            collective_id=2, has_side_effects=True, vmem_limit_bytes=VMEM_LIMIT
        ),
        name="pull",
    )(target, header, received, spectrum, edges, table_high, table_low, lines)
    return (potential[None], forces)


def solution(mesh):
    placed = (
        P(("pln", "pen"), None),
        P(("pln", "pen")),
        P(("pln", "pen")),
        P(("pln", "pen"), None),
        P(("pln", "pen"), None, None),
        P(("pln", "pen"), None),
    )
    return jax.shard_map(
        shards,
        mesh=mesh,
        in_specs=placed,
        out_specs=(P("pln", "pen", None), P(("pln", "pen"), None, None)),
        check_vma=False,
    )
```

```python
import functools
import math

import jax
import jax.numpy as jnp
import numpy as np
from jax import lax
from jax.experimental import pallas as pl
from jax.experimental.pallas import tpu as pltpu
from jax.sharding import PartitionSpec as P

NG = 1024
LANES = 128
CHUNKS = NG // LANES
screening = 2e-05
VMEM_LIMIT = 62 * 1024 * 1024
UNROLL = 8


def round_up(value, step):
    return -(-value // step) * step


@functools.lru_cache(None)
def hartley_tables():
    index = np.arange(NG)
    angle = 2.0 * np.pi / NG * (index[:, None] * index[None, :] % NG)
    table = np.cos(angle) + np.sin(angle)
    high = table.astype(jnp.bfloat16)
    low = (table - high.astype(np.float64)).astype(jnp.bfloat16)
    return high, low


@functools.lru_cache(None)
def line_tables(pen_count):
    rows = NG // pen_count
    shift = 4.0 * np.sin(np.pi * np.arange(NG) / NG) ** 2 + screening
    root = 1.0 + shift / 2.0 - np.sqrt(shift + shift * shift / 4.0)
    i = np.arange(8)[:, None]

    def power(exponent):
        return root[None, :] ** (exponent + np.zeros((8, 1)))

    tiles = [
        power(7 - i),
        power(i),
        power(8),
        np.where(i >= 1, power(1), 0.0),
        np.where(i >= 2, power(2), 0.0),
        np.where(i >= 4, power(4), 0.0),
        np.where(i <= 6, power(1), 0.0),
        np.where(i <= 5, power(2), 0.0),
        np.where(i <= 3, power(4), 0.0),
        power(i + 1),
        power(8 - i),
        np.broadcast_to(1.0 / ((1.0 / root - root) * NG), (8, NG)),
        np.broadcast_to(2.0 + shift, (8, NG)),
        power(rows - 1),
    ]
    lags = np.arange(round_up(pen_count, 8))[:, None]
    tiles.append(root[None, :] ** (lags * rows) / (1.0 - root[None, :] ** NG))
    return np.concatenate(tiles, axis=0).astype(np.float32)


T_FEND, T_BEND, T_EIGHT, T_F1, T_F2, T_F4, T_B1, T_B2, T_B4, T_FC, T_BC, T_NORM, T_DIAG, T_LAST, T_LAG = range(15)


def fetch(sources, targets, sems):
    copies = [pltpu.make_async_copy(a, b, sems.at[i]) for i, (a, b) in enumerate(zip(sources, targets))]
    for copy in copies:
        copy.start()
    return copies


def pack_kernel(capacity, owner_h, band_h, count_h, cells_h, offsets_h, charges_h, out, header, target,
                owner, band, count, cells, offsets, charges, used, sems):
    devices = out.shape[0]
    copies = fetch(
        (owner_h, band_h, count_h, cells_h, offsets_h, charges_h),
        (owner, band, count, cells, offsets, charges),
        sems,
    )
    out[...] = jnp.zeros(out.shape, jnp.float32)
    header[...] = jnp.full(header.shape, -1, jnp.int32)

    def clear(i, carry):
        used[i] = 0
        return carry

    lax.fori_loop(0, devices, clear, 0)
    lane = lax.broadcasted_iota(jnp.int32, (1, LANES), 1)
    for copy in copies:
        copy.wait()

    def place(i, carry):
        o = owner[i]
        j = used[o]
        used[o] = j + 1
        target[i] = o * capacity + j
        pair = offsets[i]
        out[o, pl.ds(j, 1), :] = pair[0:1]
        out[o, pl.ds(capacity + j, 1), :] = pair[1:2]
        out[o, pl.ds(2 * capacity + j, 1), :] = jnp.where(lane < count[i], charges[pl.ds(i, 1), :], 0.0)
        out[o, pl.ds(3 * capacity + j, 1), :] = cells[pl.ds(i, 1), :].astype(jnp.float32)
        header[o] = jnp.where(lane == j, band[i], header[o])
        return carry

    lax.fori_loop(0, owner.shape[0], place, 0)


def peer(index, pens):
    return (lax.div(index, pens), lax.rem(index, pens))


def exchange_kernel(planes, pens, arrays, *refs):
    sources, targets = refs[:arrays], refs[arrays : 2 * arrays]
    send_sems, recv_sems, own_sems = refs[2 * arrays :]
    count = planes * pens
    me = lax.axis_index("pln") * pens + lax.axis_index("pen")
    barrier = pltpu.get_barrier_semaphore()

    def greet(k, carry):
        other = peer(lax.rem(me + k, count), pens)
        pl.semaphore_signal(barrier, inc=1, device_id=other, device_id_type=pl.DeviceIdType.MESH)
        return carry

    own = [
        pltpu.make_async_copy(sources[n].at[me], targets[n].at[me], own_sems.at[n]) for n in range(arrays)
    ]
    for copy in own:
        copy.start()
    lax.fori_loop(1, count, greet, 0)
    pl.semaphore_wait(barrier, count - 1)

    def copy_of(n, k, source, target, other):
        return pltpu.make_async_remote_copy(
            src_ref=sources[n].at[source],
            dst_ref=targets[n].at[target],
            send_sem=send_sems.at[n, k],
            recv_sem=recv_sems.at[n, k],
            device_id=peer(other, pens),
            device_id_type=pl.DeviceIdType.MESH,
        )

    def send(k, carry):
        to = lax.rem(me + k, count)
        for n in range(arrays):
            copy_of(n, k, to, me, to).start()
        return carry

    def finish(k, carry):
        to = lax.rem(me + k, count)
        behind = lax.rem(me - k + count, count)
        for n in range(arrays):
            copy_of(n, k, to, me, to).wait_send()
            copy_of(n, k, me, behind, behind).wait_recv()
        return carry

    lax.fori_loop(1, count, send, 0)
    lax.fori_loop(1, count, finish, 0)
    for copy in own:
        copy.wait()


def exchange(values, planes, pens, number):
    place = pl.BlockSpec(memory_space=pl.ANY)
    arrays = len(values)
    return pl.pallas_call(
        functools.partial(exchange_kernel, planes, pens, arrays),
        out_shape=tuple(jax.ShapeDtypeStruct(v.shape, v.dtype) for v in values),
        in_specs=[place] * arrays,
        out_specs=(place,) * arrays,
        scratch_shapes=[
            pltpu.SemaphoreType.DMA((arrays, planes * pens)),
            pltpu.SemaphoreType.DMA((arrays, planes * pens)),
            pltpu.SemaphoreType.DMA((arrays,)),
        ],
        compiler_params=pltpu.CompilerParams(
            collective_id=number, has_side_effects=True, vmem_limit_bytes=VMEM_LIMIT
        ),
        name="exchange",
    )(*values)


def live_list(header, live, capacity):
    def check(d, n):
        for j in range(capacity):
            live[n] = d * capacity + j
            n = n + jnp.where(header[d, 0, j] >= 0, 1, 0)
        return n

    return lax.fori_loop(0, header.shape[0], check, jnp.int32(0))


def particle(recv, capacity, s):
    d = s // capacity
    j = s % capacity

    def spread(which):
        return recv[d, pl.ds(which * capacity + j, 8, stride=0), :]

    return factors(spread(0), spread(1), spread(2), spread(3))


def factors(frac_x, frac_y, weight, cell):
    cell = cell.astype(jnp.int32)
    column = cell & (NG - 1)
    after = (column + 1) & (NG - 1)
    row = cell >> (NG.bit_length() - 1)
    left = (1.0 - frac_x).astype(jnp.bfloat16).astype(jnp.float32)
    right = frac_x.astype(jnp.bfloat16).astype(jnp.float32)
    return frac_y, weight, row, column, after, left, right


def dot3(a_high, a_low, b_high, b_low):
    dot = functools.partial(jnp.dot, preferred_element_type=jnp.float32)
    return dot(a_high, b_high) + (dot(a_high, b_low) + dot(a_low, b_high))


def split(values):
    high = values.astype(jnp.bfloat16)
    return high, (values - high.astype(jnp.float32)).astype(jnp.bfloat16)


def deposit_kernel(capacity, rows, header_h, recv_h, table_high_h, table_low_h, lines_h, spectrum, edges,
                   live, dens, hi, lo, tails, header, recv, table_high, table_low, lines, sems):
    copies = fetch(
        (header_h, recv_h, table_high_h, table_low_h, lines_h),
        (header, recv.at[:, 0 : 4 * capacity], table_high, table_low, lines),
        sems,
    )
    dens[...] = jnp.zeros(dens.shape, jnp.float32)
    tails[...] = jnp.zeros(tails.shape, jnp.float32)
    copies[0].wait()
    n_live = live_list(header, live, capacity)
    copies[1].wait()
    sub8 = lax.broadcasted_iota(jnp.int32, (8, LANES), 0)
    places = [sub8 + 8 * b for b in range(LANES // 8)]

    def one(slot_at):
        alive = slot_at < n_live
        s = live[jnp.where(alive, slot_at, 0)]
        frac_y, weight, row, column, after, left, right = particle(recv, capacity, s)
        weight = jnp.where(alive, weight, 0.0)
        lower = (weight * (1.0 - frac_y)).astype(jnp.bfloat16).astype(jnp.float32)
        upper = (weight * frac_y).astype(jnp.bfloat16).astype(jnp.float32)
        main = jnp.where(row == sub8, lower, jnp.where(row + 1 == sub8, upper, 0.0))
        tail = jnp.where(row == 7, upper, 0.0)

        def row_side(chunk):
            tiles = [jnp.where(chunk == a, main, 0.0) for a in range(CHUNKS)]
            tiles += [jnp.where(chunk == sub8, tail, 0.0), jnp.zeros((8, LANES), jnp.float32)]
            return jnp.concatenate(tiles, axis=0).astype(jnp.bfloat16)

        def column_side(lane, factor):
            return jnp.concatenate([jnp.where(lane == b, factor, 0.0) for b in places], axis=0).astype(jnp.bfloat16)

        lhs = jnp.concatenate([row_side(column >> 7), row_side(after >> 7)], axis=1)
        rhs = jnp.concatenate([column_side(column & 127, left), column_side(after & 127, right)], axis=1)
        values = lax.dot_general(lhs, rhs, (((1,), (1,)), ((), ())), preferred_element_type=jnp.float32)
        return jnp.maximum(header[s // capacity, 0, s % capacity], 0), values

    def group(g, carry):
        results = [one(g * UNROLL + k) for k in range(UNROLL)]
        for band, values in results:
            start = pl.multiple_of(band * 8, 8)
            for a in range(CHUNKS):
                dens[pl.ds(start, 8), a * LANES : (a + 1) * LANES] += values[a * 8 : (a + 1) * 8]
            tails[band] += values[CHUNKS * 8 : CHUNKS * 8 + 8]
        return carry

    lax.fori_loop(0, (n_live + UNROLL - 1) // UNROLL, group, 0)

    def carry_row(t, carry):
        start = pl.multiple_of(t * 8 + 8, 8)
        extra = tails[t]
        for a in range(CHUNKS):
            dens[pl.ds(start, 1), a * LANES : (a + 1) * LANES] += extra[a : a + 1]
        return carry

    lax.fori_loop(0, rows // 8, carry_row, 0)
    high, low = split(dens[...])
    hi[...] = high
    lo[...] = low
    width = 256
    for copy in copies[2:]:
        copy.wait()
    for n in range(NG // width):
        cols = slice(n * width, (n + 1) * width)
        values = dot3(hi[...], lo[...], table_high[:, cols], table_low[:, cols])
        spectrum[:, cols] = values[:rows]
        edges[2:3, cols] = values[rows : rows + 1]
    eight = lines[T_EIGHT * 8 : T_EIGHT * 8 + 8]
    tiles = rows // 8

    def fold(t, carry):
        fwd, bwd = carry
        fwd = eight * fwd + spectrum[pl.ds(pl.multiple_of(t * 8, 8), 8), :]
        bwd = eight * bwd + spectrum[pl.ds(pl.multiple_of((tiles - 1 - t) * 8, 8), 8), :]
        return fwd, bwd

    nothing = jnp.zeros((8, NG), jnp.float32)
    fwd, bwd = lax.fori_loop(0, tiles, fold, (nothing, nothing))
    edges[0:1] = jnp.sum(fwd * lines[T_FEND * 8 : T_FEND * 8 + 8], axis=0, keepdims=True)
    edges[1:2] = jnp.sum(bwd * lines[T_BEND * 8 : T_BEND * 8 + 8], axis=0, keepdims=True)
    edges[3:5] = spectrum[0:2]
    edges[5:6] = spectrum[rows - 1 : rows]
    edges[6:8] = jnp.zeros((2, NG), jnp.float32)


def solve(rows, mine, copies, potential_h, out_sem, rim, wave, hi, lo, field, potential, spectrum, gathered,
          table_high, table_low, lines):
    pens = gathered.shape[0]
    def table(which):
        return lines[which * 8 : which * 8 + 8]

    def row_of(pen, which):
        return gathered[lax.rem(pen + 2 * pens, pens), which : which + 1]

    last_power = table(T_LAST)[0:1]
    before = jnp.zeros((1, NG), jnp.float32)
    beyond = jnp.zeros((1, NG), jnp.float32)
    for j in range(pens):
        lag = lines[T_LAG * 8 + j : T_LAG * 8 + j + 1]
        behind, ahead = mine - 1 - j, mine + 1 + j
        before += lag * (row_of(behind, 0) + last_power * row_of(behind - 1, 2))
        beyond += lag * (row_of(ahead, 1) + row_of(ahead - 1, 2))
    incoming = row_of(mine - 1, 2)
    next_zero = row_of(mine + 1, 3) + row_of(mine, 2)
    next_one = row_of(mine + 1, 4)
    last_before = row_of(mine - 1, 5)
    spectrum_first = spectrum[0:1] + incoming
    first_row = lax.broadcasted_iota(jnp.int32, (8, NG), 0) == 0
    tiles = rows // 8

    def tile_of(t):
        values = spectrum[pl.ds(pl.multiple_of(t * 8, 8), 8), :]
        return values + jnp.where(first_row & (t == 0), incoming, 0.0)

    def backward(i, carry):
        t = tiles - 1 - i
        x = tile_of(t)
        x = x + table(T_B1) * pltpu.roll(x, 7, 0)
        x = x + table(T_B2) * pltpu.roll(x, 6, 0)
        x = x + table(T_B4) * pltpu.roll(x, 4, 0)
        x = x + table(T_BC) * carry
        wave[pl.ds(pl.multiple_of(t * 8 + 8, 8), 8), :] = x
        return x[0:1]

    first_back = lax.fori_loop(0, tiles, backward, beyond)
    norm = table(T_NORM)[0:1]

    def forward(t, carry):
        d = tile_of(t)
        x = d + table(T_F1) * pltpu.roll(d, 1, 0)
        x = x + table(T_F2) * pltpu.roll(x, 2, 0)
        x = x + table(T_F4) * pltpu.roll(x, 4, 0)
        x = x + table(T_FC) * carry
        where = pl.ds(pl.multiple_of(t * 8 + 8, 8), 8)
        wave[where, :] = table(T_NORM) * (x + wave[where, :] - d)
        return x[7:8]

    final = lax.fori_loop(0, tiles, forward, before)
    diagonal = table(T_DIAG)[0:1]
    root = table(T_FC)[0:1]
    scale = 1.0 / NG
    up1 = norm * (before + root * first_back)
    up2 = diagonal * up1 - wave[8:9] - scale * last_before
    down0 = norm * (root * final + beyond)
    down1 = diagonal * down0 - wave[rows + 7 : rows + 8] - scale * next_zero
    down2 = diagonal * down1 - down0 - scale * next_one
    wave[0:6] = jnp.zeros((6, NG), jnp.float32)
    wave[6:7] = up2
    wave[7:8] = up1
    wave[rows + 8 : rows + 9] = down0
    wave[rows + 9 : rows + 10] = down1
    wave[rows + 10 : rows + 11] = down2
    wave[rows + 11 : rows + 16] = jnp.zeros((5, NG), jnp.float32)
    high, low = split(wave[...])
    hi[...] = high
    lo[...] = low
    width = 256
    for copy in copies:
        copy.wait()
    for n in range(NG // width):
        cols = slice(n * width, (n + 1) * width)
        wave[:, cols] = dot3(hi[...], lo[...], table_high[:, cols], table_low[:, cols])
    potential[...] = wave[8 : rows + 8]
    out_copy = pltpu.make_async_copy(potential, potential_h, out_sem)
    out_copy.start()

    def derive(t, carry):
        base = pl.multiple_of(t * 8, 8)
        tall = jnp.concatenate(
            [
                wave[pl.ds(base, 8), :],
                wave[pl.ds(pl.multiple_of(base + 8, 8), 8), :],
                wave[pl.ds(pl.multiple_of(jnp.minimum(base + 16, rows + 8), 8), 8), :],
            ],
            axis=0,
        )
        middle = tall[8:16]
        along_x = (8.0 * (pltpu.roll(middle, NG - 1, 1) - pltpu.roll(middle, 1, 1))
                   - (pltpu.roll(middle, NG - 2, 1) - pltpu.roll(middle, 2, 1))) / -12.0
        along_y = (8.0 * (tall[9:17] - tall[7:15]) - (tall[10:18] - tall[6:14])) / -12.0

        @pl.when(t < tiles)
        def _():
            field[t, 0:8, :] = along_x
            field[t, 8:16, :] = along_y

        @pl.when(t > 0)
        def _():
            for a in range(CHUNKS):
                lanes = slice(a * LANES, (a + 1) * LANES)
                rim[t - 1, 2 * a : 2 * a + 1, :] = along_x[0:1, lanes]
                rim[t - 1, 2 * a + 1 : 2 * a + 2, :] = along_y[0:1, lanes]

        return carry

    lax.fori_loop(0, tiles + 1, derive, 0)
    return out_copy


def pull_kernel(planes, pens, capacity, rows, target, header_h, recv_h, spectrum_h, edges_h, table_high_h, table_low_h,
                lines_h, potential_h, out, forces, returned, header, recv, field, rim, wave, hi, lo, potential,
                spectrum, edges, gathered, table_high, table_low, lines, sems, send_sems, recv_sems,
                edge_send_sems, edge_recv_sems):
    count = planes * pens
    me = lax.axis_index("pln") * pens + lax.axis_index("pen")
    barrier = pltpu.get_barrier_semaphore()
    copies = fetch(
        (edges_h, lines_h, spectrum_h, table_high_h, table_low_h, header_h, recv_h),
        (edges, lines, spectrum, table_high, table_low, header, recv),
        sems,
    )
    plane = lax.axis_index("pln")
    mine = lax.axis_index("pen")

    def greet(k, carry):
        other = peer(lax.rem(me + k, count), pens)
        pl.semaphore_signal(barrier, inc=1, device_id=other, device_id_type=pl.DeviceIdType.MESH)
        return carry

    lax.fori_loop(1, count, greet, 0)
    for copy in copies[:3]:
        copy.wait()
    gathered[mine] = edges[...]
    pl.semaphore_wait(barrier, count - 1)

    def edge_copy(k, place, other):
        return pltpu.make_async_remote_copy(
            src_ref=edges,
            dst_ref=gathered.at[place],
            send_sem=edge_send_sems.at[k],
            recv_sem=edge_recv_sems.at[k],
            device_id=(plane, other),
            device_id_type=pl.DeviceIdType.MESH,
        )

    for k in range(1, pens):
        edge_copy(k, mine, lax.rem(mine + k, pens)).start()
    for k in range(1, pens):
        behind = lax.rem(mine - k + pens, pens)
        edge_copy(k, mine, lax.rem(mine + k, pens)).wait_send()
        edge_copy(k, behind, behind).wait_recv()
    out_copy = solve(rows, mine, copies[3:5], potential_h, sems.at[7], rim, wave, hi, lo, field, potential, spectrum,
                     gathered, table_high, table_low, lines)
    for copy in copies[5:]:
        copy.wait()
    sub8 = lax.broadcasted_iota(jnp.int32, (8, LANES), 0)
    odd = (sub8 & 1) == 1
    pair = sub8 >> 1

    def pick(values, index):
        return jnp.take_along_axis(values, index, axis=1, mode="promise_in_bounds")

    def one(d, j):
        def spread(which):
            at = which * capacity + j
            return jnp.broadcast_to(recv[d, at : at + 1, :], (8, LANES))

        band = jnp.maximum(header[d, 0, j], 0)
        frac_y, weight, row, column, after, left, right = factors(
            spread(0), spread(1), spread(2), spread(3)
        )
        index = column & 127
        index_after = after & 127
        chunk = column >> 7
        chunk_after = after >> 7
        here = [chunk == a for a in range(1, CHUNKS)]
        there = [chunk_after == a for a in range(1, CHUNKS)]
        row_weight = weight * jnp.where(row == sub8, 1.0 - frac_y, jnp.where(row + 1 == sub8, frac_y, 0.0))
        rows_of = field[band]
        mixed = []
        for part in range(2):
            for a in range(CHUNKS):
                values = rows_of[part * 8 : part * 8 + 8, a * LANES : (a + 1) * LANES]
                g, h = pick(values, index), pick(values, index_after)
                near = g if a == 0 else jnp.where(here[a - 1], g, near)
                far = h if a == 0 else jnp.where(there[a - 1], h, far)
            mixed.append(row_weight * (left * near + right * far))
        edge = weight * jnp.where(row == 7, frac_y, 0.0)
        rims = jnp.zeros((8, LANES), jnp.float32)
        rims_of = rim[band]
        for half in range(2):
            values = rims_of[half * 8 : half * 8 + 8]
            spot = pair + half * 4
            rims += jnp.where(spot == chunk, left * pick(values, index), 0.0)
            rims += jnp.where(spot == chunk_after, right * pick(values, index_after), 0.0)
        rims = edge * rims
        return [
            jnp.sum(mixed[0] + jnp.where(odd, 0.0, rims), axis=0, keepdims=True),
            jnp.sum(mixed[1] + jnp.where(odd, rims, 0.0), axis=0, keepdims=True),
        ]

    def pull(d):
        made = [one(d, j) for j in range(capacity)]
        for c in range(2):
            for j in range(capacity):
                forces[d, c * capacity + j : c * capacity + j + 1, :] = made[j][c]
        if forces.shape[1] > 2 * capacity:
            forces[d, 2 * capacity :, :] = jnp.zeros((forces.shape[1] - 2 * capacity, LANES), jnp.float32)

    def copy_of(k, source, place, other):
        return pltpu.make_async_remote_copy(
            src_ref=forces.at[source],
            dst_ref=returned.at[place],
            send_sem=send_sems.at[k],
            recv_sem=recv_sems.at[k],
            device_id=peer(other, pens),
            device_id_type=pl.DeviceIdType.MESH,
        )

    pull(lax.rem(me + 1, count))

    def step(k, carry):
        to = lax.rem(me + k, count)
        copy_of(k, to, me, to).start()
        pull(lax.rem(me + k + 1, count))
        return carry

    lax.fori_loop(1, count, step, 0)
    returned[me] = forces[me]

    def finish(k, carry):
        to = lax.rem(me + k, count)
        behind = lax.rem(me - k + count, count)
        copy_of(k, to, me, to).wait_send()
        copy_of(k, me, behind, behind).wait_recv()
        return carry

    lax.fori_loop(1, count, finish, 0)

    def take(i, carry):
        d = target[i] // capacity
        j = target[i] % capacity
        out[i, 0:1, :] = returned[d, pl.ds(j, 1), :]
        out[i, 1:2, :] = returned[d, pl.ds(capacity + j, 1), :]
        return carry

    lax.fori_loop(0, out.shape[0], take, 0)
    out_copy.wait()


def shards(block_owner, block_band, block_count, cells, offsets, charges):
    plane_count = lax.axis_size("pln")
    pen_count = lax.axis_size("pen")
    devices = plane_count * pen_count
    local_blocks, block_len = charges.shape
    capacity = max(2, 2 * local_blocks // devices)
    total = devices * capacity
    rows = NG // pen_count
    tall = 4 * capacity
    tall_back = round_up(2 * capacity, 8)
    smem = pl.BlockSpec(memory_space=pltpu.SMEM)
    vmem = pl.BlockSpec(memory_space=pltpu.VMEM)
    far = pl.BlockSpec(memory_space=pltpu.HBM)
    params = pltpu.CompilerParams(vmem_limit_bytes=VMEM_LIMIT)
    packed, header, target = pl.pallas_call(
        functools.partial(pack_kernel, capacity),
        out_shape=(
            jax.ShapeDtypeStruct((devices, tall, LANES), jnp.float32),
            jax.ShapeDtypeStruct((devices, 1, LANES), jnp.int32),
            jax.ShapeDtypeStruct((local_blocks,), jnp.int32),
        ),
        in_specs=[far] * 6,
        out_specs=(vmem, vmem, smem),
        scratch_shapes=[pltpu.SMEM((local_blocks,), jnp.int32)] * 3
        + [
            pltpu.VMEM(cells.shape, jnp.int32),
            pltpu.VMEM(offsets.shape, jnp.float32),
            pltpu.VMEM(charges.shape, jnp.float32),
            pltpu.SMEM((devices,), jnp.int32),
            pltpu.SemaphoreType.DMA((6,)),
        ],
        compiler_params=params,
        name="pack",
    )(block_owner[:, 0], block_band, block_count, cells, offsets, charges)
    received, header = exchange((packed, header), plane_count, pen_count, 0)
    table_high, table_low = (jnp.asarray(t) for t in hartley_tables())
    lines = jnp.asarray(line_tables(pen_count))
    arrived = [
        pltpu.SMEM(header.shape, jnp.int32),
        pltpu.VMEM((devices, tall + 8, LANES), jnp.float32),
    ]
    table_scratch = [
        pltpu.VMEM((NG, NG), jnp.bfloat16),
        pltpu.VMEM((NG, NG), jnp.bfloat16),
        pltpu.VMEM(lines.shape, jnp.float32),
        pltpu.SemaphoreType.DMA((8,)),
    ]
    spectrum, edges = pl.pallas_call(
        functools.partial(deposit_kernel, capacity, rows),
        out_shape=(
            jax.ShapeDtypeStruct((rows, NG), jnp.float32),
            jax.ShapeDtypeStruct((8, NG), jnp.float32),
        ),
        in_specs=[far] * 5,
        out_specs=(vmem, vmem),
        scratch_shapes=[
            pltpu.SMEM((total + 8,), jnp.int32),
            pltpu.VMEM((rows + 8, NG), jnp.float32),
            pltpu.VMEM((rows + 8, NG), jnp.bfloat16),
            pltpu.VMEM((rows + 8, NG), jnp.bfloat16),
            pltpu.VMEM((rows // 8, 8, LANES), jnp.float32),
        ]
        + arrived
        + table_scratch,
        compiler_params=params,
        name="deposit",
    )(header, received, table_high, table_low, lines)
    potential, forces = pl.pallas_call(
        functools.partial(pull_kernel, plane_count, pen_count, capacity, rows),
        out_shape=(
            jax.ShapeDtypeStruct((rows, NG), jnp.float32),
            jax.ShapeDtypeStruct((local_blocks, 2, block_len), jnp.float32),
        ),
        in_specs=[smem] + [far] * 7,
        out_specs=(far, vmem),
        scratch_shapes=[
            pltpu.VMEM((devices, tall_back, LANES), jnp.float32),
            pltpu.VMEM((devices, tall_back, LANES), jnp.float32),
            pltpu.SMEM(header.shape, jnp.int32),
            pltpu.VMEM(received.shape, jnp.float32),
            pltpu.VMEM((rows // 8, 16, NG), jnp.float32),
            pltpu.VMEM((rows // 8, 16, LANES), jnp.float32),
            pltpu.VMEM((rows + 16, NG), jnp.float32),
            pltpu.VMEM((rows + 16, NG), jnp.bfloat16),
            pltpu.VMEM((rows + 16, NG), jnp.bfloat16),
            pltpu.VMEM((rows, NG), jnp.float32),
            pltpu.VMEM((rows, NG), jnp.float32),
            pltpu.VMEM((8, NG), jnp.float32),
            pltpu.VMEM((pen_count, 8, NG), jnp.float32),
        ]
        + table_scratch
        + [
            pltpu.SemaphoreType.DMA((devices,)),
            pltpu.SemaphoreType.DMA((devices,)),
            pltpu.SemaphoreType.DMA((pen_count,)),
            pltpu.SemaphoreType.DMA((pen_count,)),
        ],
        compiler_params=pltpu.CompilerParams(
            collective_id=2, has_side_effects=True, vmem_limit_bytes=VMEM_LIMIT
        ),
        name="pull",
    )(target, header, received, spectrum, edges, table_high, table_low, lines)
    return (potential[None], forces)


def solution(mesh):
    placed = (
        P(("pln", "pen"), None),
        P(("pln", "pen")),
        P(("pln", "pen")),
        P(("pln", "pen"), None),
        P(("pln", "pen"), None, None),
        P(("pln", "pen"), None),
    )
    return jax.shard_map(
        shards,
        mesh=mesh,
        in_specs=placed,
        out_specs=(P("pln", "pen", None), P(("pln", "pen"), None, None)),
        check_vma=False,
    )
```
